32 devices in a mesh: gen: 4 (over x, core), bank: 8 (over z, y).
Axes of the slice: x: 2, y: 2, z: 4, core: 2. Of those that a mesh axis runs over, the one named last changes fastest.
Arguments:
- latents: bfloat16 [2048, 4096], P(('gen', 'bank')), may hold values from -6 to 6
- shift: bfloat16 [2048, 4096], P(('gen', 'bank')), may hold values from -3 to 3
- scale_mod: bfloat16 [2048, 4096], P(('gen', 'bank')), may hold values from -3 to 3
- head_weight: bfloat16 [4096, 1024], P('gen'), may hold values from -0.09375 to 0.09375
- bank: bfloat16 [16384, 1024], P('bank'), may hold values from -8 to 8
Outputs:
- update: float32 [4096, 1024], P(('gen', 'bank'))
The draws below stay inside these ranges and needn't reach their ends.
All inputs are finite; a program needn't handle non-finite values.
Results may differ from the reference program's by a relative error of at most 0.0042.
Values may be sent and summed in bfloat16 or wider, within the bound.
No kernel may reach another device: no remote copies, remote signals or barrier semaphores. Data moves between devices by JAX's collectives and lax.ppermute only.
A program may use at most 128 MiB of HBM per device.

```python
import jax
import jax.numpy as jnp
from jax import lax

D = 4096
E = 1024
ROWS_DEV = 2048
BATCH = 512
SAMPLES = 2048
BANK = 16384
N_GEN = 4
N_BANK = 8


def draw_bank(key, part):
    base = jax.random.fold_in(key, 7)
    key_center, key_jitter = jax.random.split(base)
    blocks = BANK // ROWS_DEV
    centers = jax.random.normal(key_center, (blocks, 1, E), jnp.float32)
    jitter = jax.random.normal(key_jitter, (blocks, ROWS_DEV, E), jnp.float32)
    drawn = jnp.clip(centers + jitter, -8.0, 8.0).reshape(BANK, E)
    return drawn.astype(jnp.bfloat16)


def block_scale(stream_key, shape, pieces, low, top_value):
    factor_of = 1.0
    for dim, blocks in pieces:
        draws = jax.random.uniform(jax.random.fold_in(jax.random.fold_in(stream_key, 6), dim), (blocks,), jnp.float32, low / len(pieces), top_value / len(pieces))
        factor_of = factor_of * jnp.repeat(jnp.exp(draws), shape[dim] // blocks).reshape((-1,) + (1,) * (len(shape) - 1 - dim))
    return factor_of


def noise(own_key, dims, scale, bound, pieces=(), kind=jnp.bfloat16):
    values = jax.random.normal(own_key, dims, jnp.float32) * scale
    if len(pieces) > 0:
        values = block_scale(own_key, dims, pieces, -0.22, 0.18) * values
    return jnp.clip(values, min=-bound, max=bound).astype(kind)


def setup_inputs(seed: int = 0) -> dict:
    arg_keys = jax.random.split(jax.random.key(seed), 6)
    latents = noise(arg_keys[0], (SAMPLES, D), 1.0, 6.0, ((0, 32),))
    shift = noise(arg_keys[1], (SAMPLES, D), 0.5, 3.0, ((0, 32),))
    scale_mod = noise(arg_keys[2], (SAMPLES, D), 0.5, 3.0, ((0, 32),))
    head_weight = noise(arg_keys[3], (D, E), D ** -0.5, 0.09375, ((0, 4),))
    bank = draw_bank(jax.random.fold_in(arg_keys[5], 71), 0)
    return {"latents": latents, "shift": shift, "scale_mod": scale_mod, "head_weight": head_weight, "bank": bank}


kernel_scale = 32.0

def reference(latents, shift, scale_mod, head_weight, bank):
    feats = latents.astype(jnp.float32)
    inverse = lax.rsqrt(lax.optimization_barrier(jnp.mean(feats * feats, axis=1, keepdims=True)) + 1e-06)
    hidden = (feats * inverse * (1.0 + scale_mod.astype(jnp.float32)) + shift.astype(jnp.float32)).astype(jnp.bfloat16)
    embed = jnp.dot(hidden, head_weight, preferred_element_type=jnp.float32)
    length = jnp.sqrt(lax.optimization_barrier(jnp.sum(embed * embed, axis=1, keepdims=True)) + 1e-06)
    unit_exact = embed / length
    unit = unit_exact.astype(jnp.bfloat16)
    bank_f = bank.astype(jnp.float32)
    bank_unit = (bank_f / jnp.sqrt(lax.optimization_barrier(jnp.sum(bank_f * bank_f, axis=1, keepdims=True)) + 1e-06)).astype(jnp.bfloat16)
    groups = unit.reshape(N_GEN, BATCH, unit.shape[1])
    diagonal = jnp.eye(BATCH, dtype=jnp.bool_)

    def batch_term(members):
        scores = jnp.dot(members, members.T, preferred_element_type=jnp.float32)
        weights = jnp.where(diagonal, jnp.float32(0.0), jnp.exp(kernel_scale * scores)).astype(jnp.bfloat16)
        return jnp.dot(weights, members, preferred_element_type=jnp.float32)
    near = lax.map(batch_term, groups).reshape(unit.shape) / (BATCH - 1)
    blocks = bank_unit.reshape(N_BANK, ROWS_DEV, bank_unit.shape[1])

    def add_block(total, block):
        scores = jnp.dot(unit, block.T, preferred_element_type=jnp.float32)
        weights = jnp.exp(kernel_scale * scores).astype(jnp.bfloat16)
        return (total + jnp.dot(weights, block, preferred_element_type=jnp.float32), None)
    total, _ = lax.scan(add_block, jnp.zeros(unit.shape, jnp.float32), blocks)
    far = total / BANK
    proof = near - far
    radial = lax.optimization_barrier(jnp.sum(unit_exact * proof, axis=1, keepdims=True))
    grad_embed = ((proof - unit_exact * radial) / length).astype(jnp.bfloat16)
    gradient = jnp.dot(hidden.T, grad_embed, preferred_element_type=jnp.float32)
    return gradient * lax.rsqrt(jnp.mean(gradient * gradient) + 1e-06)
```

```python
import jax
import jax.numpy as jnp
from jax import lax
from jax.sharding import PartitionSpec as P

kernel_scale = 32.0


def swap(value, axis, mask):
    count = lax.axis_size(axis)
    return lax.ppermute(value, axis, [(i, i ^ mask) for i in range(count)])


def normalize(rows):
    rows = rows.astype(jnp.float32)
    return (rows / jnp.sqrt(jnp.sum(rows * rows, axis=1, keepdims=True) + 1e-06)).astype(
        jnp.bfloat16
    )


def local(latents, shift, scale_mod, head_weight, bank):
    samples, depth = latents.shape
    width = head_weight.shape[1]
    quarter = head_weight.shape[0]
    n_gen = lax.axis_size("gen")
    n_bank = lax.axis_size("bank")
    gen = lax.axis_index("gen")
    me = lax.axis_index("bank")
    side, core = gen // 2, gen % 2
    even = range(2, n_bank, 2)

    half = bank.shape[0] // 2
    bank_half = swap(lax.dynamic_slice_in_dim(bank, core * half, half, 0), "bank", 1)
    head_other = swap(head_weight, "gen", 1)

    feats = latents.astype(jnp.float32)
    inverse = lax.rsqrt(jnp.mean(feats * feats, axis=1, keepdims=True) + 1e-06)
    hidden = (
        feats * inverse * (1.0 + scale_mod.astype(jnp.float32)) + shift.astype(jnp.float32)
    ).astype(jnp.bfloat16)

    span = 2 * quarter
    lent = swap(lax.dynamic_slice_in_dim(hidden, (1 - side) * span, span, 1), "gen", 2)

    def project(block):
        own = lax.dynamic_slice_in_dim(block, core * quarter, quarter, 1)
        other = lax.dynamic_slice_in_dim(block, (1 - core) * quarter, quarter, 1)
        return jnp.dot(own, head_weight, preferred_element_type=jnp.float32) + jnp.dot(
            other, head_other, preferred_element_type=jnp.float32
        )

    own_part = project(lax.dynamic_slice_in_dim(hidden, side * span, span, 1))
    embed = own_part + swap(project(lent), "gen", 2)
    length = jnp.sqrt(jnp.sum(embed * embed, axis=1, keepdims=True) + 1e-06)
    unit_exact = embed / length
    unit = unit_exact.astype(jnp.bfloat16)

    pairs = hidden.reshape(samples, n_gen, n_bank // 2, 2 * (depth // n_gen // n_bank))
    piece = depth // n_gen // n_bank

    def pair_of(mask):
        return lax.dynamic_index_in_dim(pairs, (me ^ mask) // 2, 2, keepdims=False)

    columns = jnp.concatenate([pair_of(0)] + [swap(pair_of(m), "bank", m) for m in even], 0)
    parity = me % 2
    kept = lax.dynamic_slice_in_dim(columns, parity * piece, piece, 2)
    given = swap(lax.dynamic_slice_in_dim(columns, (1 - parity) * piece, piece, 2), "bank", 1)

    line = jnp.concatenate([unit] + [swap(unit, "bank", m) for m in even], 0)
    across = swap(line, "bank", 1)
    half_unit = normalize(bank_half)
    rows_list = [normalize(bank), half_unit, swap(half_unit, "gen", 1)]
    far_part = 0.0
    for rows in rows_list:
        scores = jnp.dot(line, rows.T, preferred_element_type=jnp.float32)
        weight = jnp.exp(kernel_scale * scores).astype(jnp.bfloat16)
        far_part = far_part + jnp.dot(weight, rows, preferred_element_type=jnp.float32)
    far = far_part[:samples]
    for i, m in enumerate(even):
        block = far_part[(i + 1) * samples : (i + 2) * samples].astype(jnp.bfloat16)
        far = far + swap(block, "bank", m).astype(jnp.float32)
    far = far / (bank.shape[0] * n_bank)

    members = jnp.concatenate([line, across], 0)
    batch = members.shape[0]
    scores = jnp.dot(unit, members.T, preferred_element_type=jnp.float32)
    same = lax.broadcasted_iota(jnp.int32, scores.shape, 0) == lax.broadcasted_iota(
        jnp.int32, scores.shape, 1
    )
    pair_weight = jnp.where(same, jnp.float32(0.0), jnp.exp(kernel_scale * scores)).astype(
        jnp.bfloat16
    )
    near = jnp.dot(pair_weight, members, preferred_element_type=jnp.float32) / (batch - 1)

    proof = near - far
    radial = jnp.sum(unit_exact * proof, axis=1, keepdims=True)
    grad_embed = ((proof - unit_exact * radial) / length).astype(jnp.bfloat16)

    odd = range(1, n_bank, 2)
    grads = [swap(grad_embed, "bank", m) for m in list(even) + list(odd)]
    grads = jnp.concatenate([grad_embed] + grads, 0)
    features = jnp.concatenate([kept, given], 0).reshape(batch, n_gen * piece)
    partial = lax.dot_general(
        features, grads, (((0,), (0,)), ((), ())), preferred_element_type=jnp.float32
    ).reshape(n_gen // 2, 2, piece, width)
    summed = lax.dynamic_index_in_dim(partial, core, 1, keepdims=False) + swap(
        lax.dynamic_index_in_dim(partial, 1 - core, 1, keepdims=False), "gen", 1
    )
    away = lax.dynamic_index_in_dim(summed, 1 - side, 0, keepdims=False).astype(jnp.bfloat16)
    gradient = lax.dynamic_index_in_dim(summed, side, 0, keepdims=False) + swap(
        away, "gen", 2
    ).astype(jnp.float32)

    squares = jnp.sum((gradient * gradient).reshape(-1, 8, 128), axis=0)
    squares = jnp.broadcast_to(jnp.sum(squares), (8, 128))
    for axis, m in [("gen", 1), ("gen", 2)] + [
        ("bank", 1 << k) for k in range(n_bank.bit_length() - 1)
    ]:
        squares = squares + swap(squares, axis, m)
    return gradient * lax.rsqrt(squares[0, 0] / (depth * width) + 1e-06)


def solution(mesh):
    placed = (
        P(("gen", "bank"), None),
        P(("gen", "bank"), None),
        P(("gen", "bank"), None),
        P("gen", None),
        P("bank", None),
    )
    return jax.shard_map(
        local, mesh=mesh, in_specs=placed, out_specs=P(("gen", "bank"), None), check_vma=False
    )
```

```python
import jax
import jax.numpy as jnp
from jax import lax
from jax.experimental import pallas as pl
from jax.experimental.pallas import tpu as pltpu
from jax.sharding import PartitionSpec as P

kernel_scale = 32.0
F32, BF16 = jnp.float32, jnp.bfloat16
SMEM = pl.BlockSpec(memory_space=pltpu.SMEM)


def swap(value, axis, mask):
    count = lax.axis_size(axis)
    return lax.ppermute(value, axis, [(i, i ^ mask) for i in range(count)])


def whole(array):
    return pl.BlockSpec(array.shape, lambda *_: (0,) * len(array.shape))


def shape(dims, dtype):
    return jax.ShapeDtypeStruct(dims, dtype)


def modulate(place, latents, shift, scale_mod):
    samples, depth = latents.shape
    rows = 16
    quarter = depth // 4

    def body(place, x_ref, b_ref, s_ref, hid_ref, lent_ref, own_ref):
        side, core = place[0], place[1]
        x = x_ref[...].astype(F32)
        inverse = lax.rsqrt(jnp.mean(x * x, axis=1, keepdims=True) + 1e-06)
        hid_ref[...] = (
            x * inverse * (1.0 + s_ref[...].astype(F32)) + b_ref[...].astype(F32)
        ).astype(BF16)
        for ref, s in ((lent_ref, 1 - side), (own_ref, side)):
            for i, c in enumerate((core, 1 - core)):
                start = pl.multiple_of((2 * s + c) * quarter, quarter)
                ref[:, i * quarter : (i + 1) * quarter] = hid_ref[:, pl.ds(start, quarter)]

    def block(width):
        return pl.BlockSpec((rows, width), lambda i: (i, 0))

    return pl.pallas_call(
        body,
        grid=(samples // rows,),
        in_specs=[SMEM] + [block(depth)] * 3,
        out_specs=[block(depth), block(depth // 2), block(depth // 2)],
        out_shape=[
            shape((samples, depth), BF16),
            shape((samples, depth // 2), BF16),
            shape((samples, depth // 2), BF16),
        ],
        cost_estimate=pl.CostEstimate(
            flops=8 * samples * depth, bytes_accessed=10 * samples * depth, transcendentals=0
        ),
        name="modulate",
    )(place, latents, shift, scale_mod)


def project(block, first, second):
    samples = block.shape[0]
    quarter, width = first.shape
    tile = quarter // 2

    def body(x_ref, w_ref, v_ref, o_ref):
        i = pl.program_id(0)

        @pl.when(i == 0)
        def _():
            o_ref[...] = jnp.zeros_like(o_ref)

        x = x_ref[:, pl.ds(pl.multiple_of(i * tile, tile), tile)]
        y = x_ref[:, pl.ds(pl.multiple_of(quarter + i * tile, tile), tile)]
        o_ref[...] += jnp.dot(x, w_ref[...], preferred_element_type=F32) + jnp.dot(
            y, v_ref[...], preferred_element_type=F32
        )

    return pl.pallas_call(
        body,
        grid=(quarter // tile,),
        in_specs=[whole(block)] + [pl.BlockSpec((tile, width), lambda i: (i, 0))] * 2,
        out_specs=pl.BlockSpec((samples, width), lambda i: (0, 0)),
        out_shape=shape((samples, width), F32),
        cost_estimate=pl.CostEstimate(
            flops=4 * samples * quarter * width,
            bytes_accessed=4 * quarter * width + 8 * samples * width,
            transcendentals=0,
        ),
        name="project",
    )(block, first, second)


def finish_embed(part, other):
    def body(a_ref, b_ref, exact_ref, unit_ref, length_ref):
        embed = a_ref[...] + b_ref[...].astype(F32)
        length = jnp.sqrt(jnp.sum(embed * embed, axis=1, keepdims=True) + 1e-06)
        exact = embed / length
        exact_ref[...] = exact
        unit_ref[...] = exact.astype(BF16)
        length_ref[...] = jnp.broadcast_to(length, length_ref.shape)

    samples, width = part.shape
    return pl.pallas_call(
        body,
        out_shape=[
            shape((samples, width), F32),
            shape((samples, width), BF16),
            shape((samples, 128), F32),
        ],
        cost_estimate=pl.CostEstimate(
            flops=6 * samples * width, bytes_accessed=14 * samples * width, transcendentals=0
        ),
        name="finish_embed",
    )(part, other)


def bank_sums(pieces, bank_unit, first_dtype):
    samples, width = pieces[0].shape
    count = len(pieces)
    total = count * samples
    tile = min(512, bank_unit.shape[0])

    def body(*refs):
        ins, rows_ref, outs = refs[:count], refs[count], refs[count + 1 : 2 * count + 1]
        held, sums = refs[2 * count + 1 :]
        step = pl.program_id(0)

        @pl.when(step == 0)
        def _():
            for i in range(count):
                held[i * samples : (i + 1) * samples] = ins[i][...]
            sums[...] = jnp.zeros_like(sums)

        rows = rows_ref[...]
        scores = lax.dot_general(
            held[...], rows, (((1,), (1,)), ((), ())), preferred_element_type=F32
        )
        weight = jnp.exp(kernel_scale * scores).astype(BF16)
        sums[...] += jnp.dot(weight, rows, preferred_element_type=F32)

        @pl.when(step == pl.num_programs(0) - 1)
        def _():
            for i in range(count):
                outs[i][...] = sums[i * samples : (i + 1) * samples].astype(outs[i].dtype)

    return pl.pallas_call(
        body,
        grid=(bank_unit.shape[0] // tile,),
        in_specs=[whole(p) for p in pieces] + [pl.BlockSpec((tile, width), lambda i: (i, 0))],
        out_specs=[whole(p) for p in pieces],
        out_shape=[
            shape((samples, width), first_dtype if i == 0 else BF16) for i in range(count)
        ],
        scratch_shapes=[pltpu.VMEM((total, width), BF16), pltpu.VMEM((total, width), F32)],
        cost_estimate=pl.CostEstimate(
            flops=4 * total * width * bank_unit.shape[0],
            bytes_accessed=2 * bank_unit.size + 6 * total * width,
            transcendentals=total * bank_unit.shape[0],
        ),
        name="bank_sums",
    )(*pieces, bank_unit)


def pair_sums(unit, others):
    samples, width = unit.shape
    count = len(others)
    batch = (count + 1) * samples

    def body(*refs):
        unit_ref, ins, out_ref, held = refs[0], refs[1 : count + 1], refs[-2], refs[-1]
        held[:samples] = unit_ref[...]
        for i in range(count):
            held[(i + 1) * samples : (i + 2) * samples] = ins[i][...]
        scores = lax.dot_general(
            unit_ref[...], held[...], (((1,), (1,)), ((), ())), preferred_element_type=F32
        )
        same = lax.broadcasted_iota(jnp.int32, scores.shape, 0) == lax.broadcasted_iota(
            jnp.int32, scores.shape, 1
        )
        weight = jnp.where(same, 0.0, jnp.exp(kernel_scale * scores)).astype(BF16)
        out_ref[...] = jnp.dot(weight, held[...], preferred_element_type=F32) / (batch - 1)

    return pl.pallas_call(
        body,
        out_shape=shape((samples, width), F32),
        scratch_shapes=[pltpu.VMEM((batch, width), BF16)],
        cost_estimate=pl.CostEstimate(
            flops=4 * samples * width * batch,
            bytes_accessed=2 * batch * width + 6 * samples * width,
            transcendentals=samples * batch,
        ),
        name="pair_sums",
    )(unit, *others)


def embed_gradient(near, far, parts, exact, length, bank_rows):
    count = len(parts)

    def body(*refs):
        near_ref, far_ref, exact_ref, length_ref = refs[:4]
        total = far_ref[...]
        for ref in refs[4 : 4 + count]:
            total = total + ref[...].astype(F32)
        proof = near_ref[...] - total / bank_rows
        exact = exact_ref[...]
        radial = jnp.sum(exact * proof, axis=1, keepdims=True)
        refs[-1][...] = ((proof - exact * radial) / length_ref[:, :1]).astype(BF16)

    samples, width = near.shape
    return pl.pallas_call(
        body,
        out_shape=shape((samples, width), BF16),
        cost_estimate=pl.CostEstimate(
            flops=(count + 8) * samples * width,
            bytes_accessed=(14 + 2 * count) * samples * width,
            transcendentals=0,
        ),
        name="embed_gradient",
    )(near, far, exact, length, *parts)


def feature_sums(place, columns, grads, away):
    samples, width = grads[0].shape
    count = len(grads)
    piece = columns.shape[0] // 4

    def body(*refs):
        place, cols_ref = refs[0], refs[1]
        ins, outs, held = refs[2 : 2 + count], refs[2 + count : 4 + count], refs[-1]
        side, core = place[0], place[1]
        for i in range(count):
            held[i * samples : (i + 1) * samples] = ins[i][...]
        s = 1 - side if away else side
        for ref, c in zip(outs, (1 - core, core)):
            start = pl.multiple_of((2 * s + c) * piece, piece)
            ref[...] = jnp.dot(
                cols_ref[pl.ds(start, piece), :], held[...], preferred_element_type=F32
            )

    return pl.pallas_call(
        body,
        in_specs=[SMEM] + [whole(columns)] + [whole(g) for g in grads],
        out_shape=[shape((piece, width), F32)] * 2,
        scratch_shapes=[pltpu.VMEM((count * samples, width), BF16)],
        cost_estimate=pl.CostEstimate(
            flops=4 * piece * width * count * samples,
            bytes_accessed=2 * columns.size + 2 * count * samples * width + 8 * piece * width,
            transcendentals=0,
        ),
        name="feature_sums",
    )(place, columns, *grads)


def square_sums(kept, from_core, from_side, devices):
    rows, width = kept.shape

    def body(a_ref, b_ref, c_ref, grad_ref, out_ref):
        grad = a_ref[...] + b_ref[...] + c_ref[...].astype(F32)
        grad_ref[...] = grad
        squares = jnp.sum((grad * grad).reshape(rows // 8, 8, width), axis=0)
        tile = squares[:, :128]
        for i in range(1, width // 128):
            tile = tile + squares[:, i * 128 : (i + 1) * 128]
        out_ref[...] = jnp.broadcast_to(tile[None], out_ref.shape)

    return pl.pallas_call(
        body,
        out_shape=[shape((rows, width), F32), shape((devices, 8, 128), F32)],
        cost_estimate=pl.CostEstimate(
            flops=4 * rows * width, bytes_accessed=14 * rows * width, transcendentals=0
        ),
        name="square_sums",
    )(kept, from_core, from_side)


def scaled(gradient, squares, entries):
    def body(g_ref, s_ref, o_ref):
        mean = jnp.sum(s_ref[...]) / entries
        o_ref[...] = g_ref[...] * lax.rsqrt(jnp.full((1, 1), mean + 1e-06, F32))

    return pl.pallas_call(
        body,
        out_shape=shape(gradient.shape, F32),
        cost_estimate=pl.CostEstimate(
            flops=gradient.size, bytes_accessed=8 * gradient.size, transcendentals=1
        ),
        name="scaled",
    )(gradient, squares)


def local(latents, shift, scale_mod, head_weight, bank):
    samples, depth = latents.shape
    width = head_weight.shape[1]
    n_gen = lax.axis_size("gen")
    n_bank = lax.axis_size("bank")
    gen = lax.axis_index("gen")
    me = lax.axis_index("bank")
    place = jnp.stack([gen // 2, gen % 2]).astype(jnp.int32)
    low = list(range(n_bank // 2))
    high = list(range(n_bank // 2, n_bank))
    evens, odds = list(range(0, n_bank, 2)), list(range(1, n_bank, 2))

    head_other = swap(head_weight, "gen", 1)
    hidden, lent, own = modulate(place, latents, shift, scale_mod)
    lent = swap(lent, "gen", 2)
    own_part = project(own, head_weight, head_other)
    returned = swap(project(lent, head_weight, head_other), "gen", 2)
    exact, unit, length = finish_embed(own_part, returned)

    piece = depth // n_gen // n_bank
    pairs = hidden.reshape(samples, n_gen, n_bank // 2, 2 * piece)

    def pair_of(mask):
        return lax.dynamic_index_in_dim(pairs, (me ^ mask) // 2, 2, keepdims=False)

    columns = jnp.concatenate([pair_of(0)] + [swap(pair_of(m), "bank", m) for m in evens[1:]], 0)
    parity = me % 2
    kept = lax.dynamic_slice_in_dim(columns, parity * piece, piece, 2)
    given = swap(lax.dynamic_slice_in_dim(columns, (1 - parity) * piece, piece, 2), "bank", 1)
    columns = jnp.concatenate([kept, given], 0).reshape(n_bank * samples, n_gen * piece).T

    bank_f = bank.astype(F32)
    bank_unit = (
        bank_f / jnp.sqrt(jnp.sum(bank_f * bank_f, axis=1, keepdims=True) + 1e-06)
    ).astype(BF16)
    members = {0: unit}
    for m in high[::-1] + low[:0:-1]:
        members[m] = swap(unit, "bank", m)
    far_low = bank_sums([members[m] for m in low], bank_unit, F32)
    far_high = bank_sums([members[m] for m in high], bank_unit, BF16)
    parts = [swap(v, "bank", m) for m, v in list(zip(high, far_high))[::-1]]
    parts += [swap(v, "bank", m) for m, v in list(zip(low, far_low))[:0:-1]]
    near = pair_sums(unit, [members[m] for m in low[1:] + high])
    grad_embed = embed_gradient(near, far_low[0], parts, exact, length, bank.shape[0] * n_bank)

    grads = {0: grad_embed}
    for m in high[::-1] + low[:0:-1]:
        grads[m] = swap(grad_embed, "bank", m)
    grads = [grads[m] for m in evens + odds]
    for_core, ours = feature_sums(place, columns, grads, True)
    away = (ours + swap(for_core, "gen", 1)).astype(BF16)
    for_core, ours = feature_sums(place, columns, grads, False)
    gradient, squares = square_sums(
        ours, swap(for_core, "gen", 1), swap(away, "gen", 2), n_gen * n_bank
    )
    squares = lax.all_to_all(squares, ("gen", "bank"), 0, 0, tiled=True)
    return scaled(gradient, squares, depth * width)


def solution(mesh):
    placed = (
        P(("gen", "bank"), None),
        P(("gen", "bank"), None),
        P(("gen", "bank"), None),
        P("gen", None),
        P("bank", None),
    )
    return jax.shard_map(
        local, mesh=mesh, in_specs=placed, out_specs=P(("gen", "bank"), None), check_vma=False
    )
```

```python
import jax
import jax.numpy as jnp
from jax import lax
from jax.experimental import pallas as pl
from jax.experimental.pallas import tpu as pltpu
from jax.sharding import PartitionSpec as P

kernel_scale = 32.0
F32, BF16 = jnp.float32, jnp.bfloat16
SMEM = pl.BlockSpec(memory_space=pltpu.SMEM)
VMEM = pl.BlockSpec(memory_space=pltpu.VMEM)
HBM = pl.BlockSpec(memory_space=pltpu.HBM)


def swap(value, axis, mask):
    count = lax.axis_size(axis)
    return lax.ppermute(value, axis, [(i, i ^ mask) for i in range(count)])


def call(body, scalars, arrays, outs, flops, scratch=(), to_hbm=False, from_hbm=False):
    space = pltpu.HBM if from_hbm else pltpu.VMEM
    arrays = [pltpu.with_memory_space_constraint(a, space) for a in arrays]
    make = jax.ShapeDtypeStruct if to_hbm else pltpu.VMEM
    size = sum(a.size * a.dtype.itemsize for a in arrays)
    head = [] if scalars is None else [scalars]
    return pl.pallas_call(
        body,
        in_specs=[SMEM] * len(head) + [HBM if from_hbm else VMEM] * len(arrays),
        out_specs=[VMEM] * len(outs),
        out_shape=[make(dims, dtype) for dims, dtype in outs],
        scratch_shapes=list(scratch),
        compiler_params=pltpu.CompilerParams(vmem_limit_bytes=24 << 20),
        cost_estimate=pl.CostEstimate(flops=flops, bytes_accessed=size, transcendentals=0),
    )(*head, *arrays)


def modulate(place, latents, shift, scale_mod):
    samples, depth = latents.shape
    rows = 16
    quarter = depth // 4
    steps = samples // rows

    def body(place, x_hbm, b_hbm, s_hbm, hid_ref, lent_ref, own_ref, x_ref, b_ref, s_ref, sems):
        side, core = place[0], place[1]
        copies = [
            [
                pltpu.make_async_copy(src.at[pl.ds(r * rows, rows)], dst.at[r], sems.at[i, r])
                for i, (src, dst) in enumerate(
                    ((x_hbm, x_ref), (b_hbm, b_ref), (s_hbm, s_ref))
                )
            ]
            for r in range(steps)
        ]
        for group in copies:
            for copy in group:
                copy.start()
        for r in range(steps):
            for copy in copies[r]:
                copy.wait()
            at = slice(r * rows, (r + 1) * rows)
            x = x_ref[r].astype(F32)
            inverse = lax.rsqrt(jnp.mean(x * x, axis=1, keepdims=True) + 1e-06)
            hid_ref[at] = (
                x * inverse * (1.0 + s_ref[r].astype(F32)) + b_ref[r].astype(F32)
            ).astype(BF16)
        for ref, s in ((lent_ref, 1 - side), (own_ref, side)):
            for i, c in enumerate((core, 1 - core)):
                start = pl.multiple_of((2 * s + c) * quarter, quarter)
                ref[:, i * quarter : (i + 1) * quarter] = hid_ref[:, pl.ds(start, quarter)]

    half = (samples, depth // 2)
    return call(
        body,
        place,
        [latents, shift, scale_mod],
        [((samples, depth), BF16), (half, BF16), (half, BF16)],
        8 * samples * depth,
        [pltpu.VMEM((steps, rows, depth), BF16)] * 3 + [pltpu.SemaphoreType.DMA((3, steps))],
        from_hbm=True,
    )


def project(block, first, second):
    samples = block.shape[0]
    quarter, width = first.shape

    def body(x_ref, w_ref, v_ref, o_ref):
        o_ref[...] = jnp.dot(
            x_ref[:, :quarter], w_ref[...], preferred_element_type=F32
        ) + jnp.dot(x_ref[:, quarter:], v_ref[...], preferred_element_type=F32)

    return call(
        body, None, [block, first, second], [((samples, width), F32)], 4 * samples * quarter * width
    )[0]


def finish_embed(part, other):
    def body(a_ref, b_ref, exact_ref, unit_ref, length_ref):
        embed = a_ref[...] + b_ref[...].astype(F32)
        length = jnp.sqrt(jnp.sum(embed * embed, axis=1, keepdims=True) + 1e-06)
        exact = embed / length
        exact_ref[...] = exact
        unit_ref[...] = exact.astype(BF16)
        length_ref[...] = jnp.broadcast_to(length, length_ref.shape)

    samples, width = part.shape
    return call(
        body,
        None,
        [part, other],
        [((samples, width), F32), ((samples, width), BF16), ((samples, 128), F32)],
        6 * samples * width,
    )


def shares(rows):
    return 9 * rows // 64, 14 * rows // 64


def prepare(place, bank, weight):
    rows, width = bank.shape
    steps = 8
    tile = rows // steps
    forward, direct = shares(rows)

    def body(place, x_hbm, w_hbm, o_ref, f_ref, d_ref, w_ref, x_ref, sems):
        copies = [
            pltpu.make_async_copy(x_hbm.at[pl.ds(i * tile, tile)], x_ref.at[i], sems.at[i])
            for i in range(steps)
        ] + [pltpu.make_async_copy(w_hbm, w_ref, sems.at[steps])]
        for copy in copies:
            copy.start()
        for i in range(steps):
            copies[i].wait()
            x = x_ref[i].astype(F32)
            o_ref[i * tile : (i + 1) * tile] = (
                x / jnp.sqrt(jnp.sum(x * x, axis=1, keepdims=True) + 1e-06)
            ).astype(BF16)
        start = pl.multiple_of((2 * place[0] + place[1]) * forward, 16)
        f_ref[...] = o_ref[pl.ds(start, forward), :]
        start = pl.multiple_of(4 * forward + place[1] * direct, 16)
        d_ref[...] = o_ref[pl.ds(start, direct), :]
        copies[steps].wait()

    return call(
        body,
        place,
        [bank, weight],
        [
            (bank.shape, BF16),
            ((forward, width), BF16),
            ((direct, width), BF16),
            (weight.shape, BF16),
        ],
        8 * bank.size,
        [pltpu.VMEM((steps, tile, width), BF16), pltpu.SemaphoreType.DMA((steps + 1,))],
        from_hbm=True,
    )


def join(pieces):
    samples, width = pieces[0].shape
    count = len(pieces)

    def body(*refs):
        for i in range(count):
            refs[-1][i * samples : (i + 1) * samples] = refs[i][...]

    return call(body, None, pieces, [((count * samples, width), BF16)], 0)[0]


def bank_sums(line, blocks, before=None, samples=None):
    total, width = line.shape
    count = 1 if samples is None else total // samples

    def body(*refs):
        line_ref, rest = refs[0], refs[1:]
        row_refs, rest = rest[: len(blocks)], rest[len(blocks) :]
        outs, sums = rest[-1 - count : -1], rest[-1]
        started = before is not None
        if started:
            sums[...] = rest[0][...]
        for block, ref in zip(blocks, row_refs):
            tile = min(512, block.shape[0])
            for start in range(0, block.shape[0], tile):
                rows = ref[start : start + tile]
                scores = lax.dot_general(
                    line_ref[...], rows, (((1,), (1,)), ((), ())), preferred_element_type=F32
                )
                weight = jnp.exp(kernel_scale * scores).astype(BF16)
                term = jnp.dot(weight, rows, preferred_element_type=F32)
                sums[...] = sums[...] + term if started else term
                started = True
        for i, ref in enumerate(outs):
            size = total // count
            ref[...] = sums[i * size : (i + 1) * size].astype(ref.dtype)

    dims = (total // count, width)
    return call(
        body,
        None,
        [line] + list(blocks) + ([] if before is None else [before]),
        [(dims, BF16 if i else F32) for i in range(count)],
        4 * total * width * sum(block.shape[0] for block in blocks),
        [pltpu.VMEM((total, width), F32)],
    )


def pair_sums(unit, line, across):
    samples, width = unit.shape
    batch = 2 * line.shape[0]

    def body(unit_ref, line_ref, across_ref, out_ref):
        total = 0.0
        for ref, first in ((line_ref, True), (across_ref, False)):
            scores = lax.dot_general(
                unit_ref[...], ref[...], (((1,), (1,)), ((), ())), preferred_element_type=F32
            )
            weight = jnp.exp(kernel_scale * scores)
            if first:
                same = lax.broadcasted_iota(
                    jnp.int32, scores.shape, 0
                ) == lax.broadcasted_iota(jnp.int32, scores.shape, 1)
                weight = jnp.where(same, 0.0, weight)
            total = total + jnp.dot(
                weight.astype(BF16), ref[...], preferred_element_type=F32
            )
        out_ref[...] = total / (batch - 1)

    return call(
        body, None, [unit, line, across], [((samples, width), F32)], 4 * samples * width * batch
    )[0]


def embed_gradient(near, far, parts, exact, length, bank_rows):
    count = len(parts)

    def body(*refs):
        near_ref, far_ref, exact_ref, length_ref = refs[:4]
        total = far_ref[...]
        for ref in refs[4 : 4 + count]:
            total = total + ref[...].astype(F32)
        proof = near_ref[...] - total / bank_rows
        exact = exact_ref[...]
        radial = jnp.sum(exact * proof, axis=1, keepdims=True)
        refs[-1][...] = ((proof - exact * radial) / length_ref[:, :1]).astype(BF16)

    samples, width = near.shape
    return call(
        body,
        None,
        [near, far, exact, length] + list(parts),
        [((samples, width), BF16)],
        (count + 8) * samples * width,
    )[0]


def spread(place, hidden, n_bank):
    samples, depth = hidden.shape
    pair = depth // 4 // n_bank * 2

    def body(place, hid_ref, *outs):
        for i, ref in enumerate(outs):
            for g in range(4):
                start = pl.multiple_of(g * (depth // 4) + (place[2] ^ i) * pair, pair)
                ref[:, g * pair : (g + 1) * pair] = hid_ref[:, pl.ds(start, pair)]

    return call(body, place, [hidden], [((samples, 4 * pair), BF16)] * (n_bank // 2), 0)


def split_pairs(place, pieces):
    samples, width = pieces[0].shape
    block = width // 8
    count = len(pieces)

    def body(place, *refs):
        ins, outs = refs[:count], refs[count:]
        for out, y in zip(outs, (place[3], 1 - place[3])):
            for i, ref in enumerate(ins):
                for g in range(4):
                    start = pl.multiple_of((2 * g + y) * block, block)
                    out[i * samples : (i + 1) * samples, g * block : (g + 1) * block] = ref[
                        :, pl.ds(start, block)
                    ]

    return call(body, place, pieces, [((count * samples, 4 * block), BF16)] * 2, 0)


def turn(kept, given):
    rows, width = kept.shape

    def body(a_ref, b_ref, o_ref):
        o_ref[:, :rows] = a_ref[...].T
        o_ref[:, rows:] = b_ref[...].T

    return call(body, None, [kept, given], [((width, 2 * rows), BF16)], 0)[0]


def feature_sums(place, columns, grads, away):
    samples, width = grads[0].shape
    count = len(grads)
    piece = columns.shape[0] // 4

    def body(place, cols_ref, *refs):
        ins, outs, held = refs[:count], refs[count : count + 2], refs[-1]
        side, core = place[0], place[1]
        for i in range(count):
            held[i * samples : (i + 1) * samples] = ins[i][...]
        s = 1 - side if away else side
        for ref, c in zip(outs, (1 - core, core)):
            start = pl.multiple_of((2 * s + c) * piece, piece)
            ref[...] = jnp.dot(
                cols_ref[pl.ds(start, piece), :], held[...], preferred_element_type=F32
            )

    return call(
        body,
        place,
        [columns] + list(grads),
        [((piece, width), F32)] * 2,
        4 * piece * width * count * samples,
        [pltpu.VMEM((count * samples, width), BF16)],
    )


def add_round(a, b):
    def body(a_ref, b_ref, o_ref):
        o_ref[...] = (a_ref[...] + b_ref[...]).astype(BF16)

    return call(body, None, [a, b], [(a.shape, BF16)], a.size)[0]


def square_sums(kept, from_core, from_side, devices):
    rows, width = kept.shape

    def body(a_ref, b_ref, c_ref, grad_ref, out_ref):
        grad = a_ref[...] + b_ref[...] + c_ref[...].astype(F32)
        grad_ref[...] = grad
        squares = jnp.sum((grad * grad).reshape(rows // 8, 8, width), axis=0)
        tile = squares[:, :128]
        for i in range(1, width // 128):
            tile = tile + squares[:, i * 128 : (i + 1) * 128]
        out_ref[...] = jnp.broadcast_to(tile[None], out_ref.shape)

    return call(
        body,
        None,
        [kept, from_core, from_side],
        [((rows, width), F32), ((devices, 8, 128), F32)],
        4 * rows * width,
    )


def scaled(gradient, squares, entries):
    def body(g_ref, s_ref, o_ref):
        mean = jnp.sum(s_ref[...]) / entries
        o_ref[...] = g_ref[...] * lax.rsqrt(jnp.full((1, 1), mean + 1e-06, F32))

    return call(
        body, None, [gradient, squares], [(gradient.shape, F32)], gradient.size, (), True
    )[0]


def by_feature(place, hidden, n_bank):
    samples, depth = hidden.shape
    piece = depth // 4 // n_bank
    if piece % 128 == 0:
        pieces = spread(place, hidden, n_bank)
        pieces = [swap(p, "bank", 2 * i) if i else p for i, p in enumerate(pieces)]
        kept, given = split_pairs(place, pieces)
        return turn(kept, swap(given, "bank", 1))
    pairs = hidden.reshape(samples, 4, n_bank // 2, 2 * piece)
    pieces = [
        lax.dynamic_index_in_dim(pairs, place[2] ^ i, 2, keepdims=False)
        for i in range(n_bank // 2)
    ]
    pieces = [swap(p, "bank", 2 * i) if i else p for i, p in enumerate(pieces)]
    columns = jnp.concatenate(pieces, 0)
    kept = lax.dynamic_slice_in_dim(columns, place[3] * piece, piece, 2)
    given = swap(lax.dynamic_slice_in_dim(columns, (1 - place[3]) * piece, piece, 2), "bank", 1)
    return jnp.concatenate([kept, given], 0).reshape(n_bank * samples, 4 * piece).T


def local(latents, shift, scale_mod, head_weight, bank):
    samples, depth = latents.shape
    width = head_weight.shape[1]
    n_gen = lax.axis_size("gen")
    n_bank = lax.axis_size("bank")
    gen = lax.axis_index("gen")
    me = lax.axis_index("bank")
    place = jnp.stack([gen // 2, gen % 2, me // 2, me % 2]).astype(jnp.int32)
    evens, odds = list(range(0, n_bank, 2)), list(range(1, n_bank, 2))

    head_other = swap(head_weight, "gen", 1)
    hidden, lent, own = modulate(place, latents, shift, scale_mod)
    bank, head_weight, lent = lax.optimization_barrier((bank, head_weight, lent))
    lent = swap(lent, "gen", 2)
    bank_unit, forward, direct, head_weight = prepare(place, bank, head_weight)
    own_part = project(own, head_weight, head_other)
    returned = swap(project(lent, head_weight, head_other), "gen", 2)
    exact, unit, length = finish_embed(own_part, returned)

    columns = by_feature(place, hidden, n_bank)

    forward = swap(forward, "bank", 1)
    direct = swap(direct, "bank", 1)
    beside = swap(forward, "gen", 2)
    early = [forward, swap(forward, "gen", 1)]
    late = [beside, direct]
    late += [swap(v, "gen", 1) for v in late]

    line = [unit] + [swap(unit, "bank", m) for m in evens[1:]]
    line = join(line)
    across = swap(line, "bank", 1)
    sums = bank_sums(line, [bank_unit])[0]
    sums = bank_sums(line, early, sums)[0]
    far = bank_sums(line, late, sums, samples)
    parts = [swap(v, "bank", m) for m, v in zip(evens[1:], far[1:])]
    near = pair_sums(unit, line, across)
    grad_embed = embed_gradient(near, far[0], parts, exact, length, bank.shape[0] * n_bank)

    grads = {0: grad_embed}
    for m in range(n_bank - 1, 0, -1):
        grads[m] = swap(grad_embed, "bank", m)
    grads = [grads[m] for m in evens + odds]
    for_core, ours = feature_sums(place, columns, grads, True)
    away = add_round(ours, swap(for_core, "gen", 1))
    for_core, ours = feature_sums(place, columns, grads, False)
    gradient, squares = square_sums(
        ours, swap(for_core, "gen", 1), swap(away, "gen", 2), n_gen * n_bank
    )
    squares = lax.all_to_all(squares, ("gen", "bank"), 0, 0, tiled=True)
    return scaled(gradient, squares, depth * width)


def solution(mesh):
    placed = (
        P(("gen", "bank"), None),
        P(("gen", "bank"), None),
        P(("gen", "bank"), None),
        P("gen", None),
        P("bank", None),
    )
    return jax.shard_map(
        lambda *args: local(*args),
        mesh=mesh,
        in_specs=placed,
        out_specs=P(("gen", "bank"), None),
        check_vma=False,
    )
```

```python
import jax
import jax.numpy as jnp
from jax import lax
from jax.experimental import pallas as pl
from jax.experimental.pallas import tpu as pltpu
from jax.sharding import PartitionSpec as P

kernel_scale = 32.0
F32, BF16 = jnp.float32, jnp.bfloat16
SMEM = pl.BlockSpec(memory_space=pltpu.SMEM)
VMEM = pl.BlockSpec(memory_space=pltpu.VMEM)
HBM = pl.BlockSpec(memory_space=pltpu.HBM)


def swap(value, axis, mask):
    count = lax.axis_size(axis)
    return lax.ppermute(value, axis, [(i, i ^ mask) for i in range(count)])


def call(body, scalars, arrays, outs, flops, scratch=(), to_hbm=False, from_hbm=0):
    far_away = [i >= len(arrays) - from_hbm for i in range(len(arrays))]
    arrays = [
        pltpu.with_memory_space_constraint(a, pltpu.HBM if there else pltpu.VMEM)
        for a, there in zip(arrays, far_away)
    ]
    make = jax.ShapeDtypeStruct if to_hbm else pltpu.VMEM
    size = sum(a.size * a.dtype.itemsize for a in arrays)
    head = [] if scalars is None else [scalars]
    return pl.pallas_call(
        body,
        in_specs=[SMEM] * len(head) + [HBM if there else VMEM for there in far_away],
        out_specs=[HBM if to_hbm else VMEM] * len(outs),
        out_shape=[make(dims, dtype) for dims, dtype in outs],
        scratch_shapes=list(scratch),
        compiler_params=pltpu.CompilerParams(vmem_limit_bytes=24 << 20),
        cost_estimate=pl.CostEstimate(flops=flops, bytes_accessed=size, transcendentals=0),
    )(*head, *arrays)


def modulate(place, latents, shift, scale_mod, bank):
    samples, depth = latents.shape
    rows = 16
    quarter = depth // 4
    steps = samples // rows
    forward, direct = shares(bank.shape[0])

    def body(place, *refs):
        sources, bank_hbm = refs[:3], refs[3]
        hid_ref, lent_ref, own_ref, f_ref, d_ref = refs[4:9]
        held, sems, row_sems = refs[9:12], refs[12], refs[13]
        side, core = place[0], place[1]
        copies = [
            [
                pltpu.make_async_copy(src.at[pl.ds(r * rows, rows)], dst.at[r], sems.at[i, r])
                for i, (src, dst) in enumerate(zip(sources, held))
            ]
            for r in range(steps)
        ]
        starts = (2 * side + core) * forward, 4 * forward + core * direct
        sent = [
            pltpu.make_async_copy(
                bank_hbm.at[pl.ds(pl.multiple_of(start, 16), ref.shape[0])], ref, row_sems.at[i]
            )
            for i, (start, ref) in enumerate(zip(starts, (f_ref, d_ref)))
        ]
        for group in copies + [sent]:
            for copy in group:
                copy.start()
        for r in range(steps):
            for copy in copies[r]:
                copy.wait()
            at = slice(r * rows, (r + 1) * rows)
            x, b, s = (ref[r].astype(F32) for ref in held)
            inverse = lax.rsqrt(jnp.mean(x * x, axis=1, keepdims=True) + 1e-06)
            hid_ref[at] = (x * inverse * (1.0 + s) + b).astype(BF16)
        for ref, s in ((lent_ref, 1 - side), (own_ref, side)):
            for i, c in enumerate((core, 1 - core)):
                start = pl.multiple_of((2 * s + c) * quarter, quarter)
                ref[:, i * quarter : (i + 1) * quarter] = hid_ref[:, pl.ds(start, quarter)]
        for copy in sent:
            copy.wait()

    half = (samples, depth // 2)
    width = bank.shape[1]
    return call(
        body,
        place,
        [latents, shift, scale_mod, bank],
        [
            ((samples, depth), BF16),
            (half, BF16),
            (half, BF16),
            ((forward, width), BF16),
            ((direct, width), BF16),
        ],
        8 * samples * depth,
        [pltpu.VMEM((steps, rows, depth), BF16)] * 3
        + [pltpu.SemaphoreType.DMA((3, steps)), pltpu.SemaphoreType.DMA((2,))],
        from_hbm=4,
    )


def project(block, first, second):
    samples = block.shape[0]
    quarter, width = first.shape

    def body(x_ref, w_ref, v_ref, o_ref):
        o_ref[...] = jnp.dot(
            x_ref[:, :quarter], w_ref[...], preferred_element_type=F32
        ) + jnp.dot(x_ref[:, quarter:], v_ref[...], preferred_element_type=F32)

    return call(
        body, None, [block, first, second], [((samples, width), F32)], 4 * samples * quarter * width
    )[0]


def finish_embed(part, other):
    def body(a_ref, b_ref, exact_ref, unit_ref, length_ref):
        embed = a_ref[...] + b_ref[...].astype(F32)
        length = jnp.sqrt(jnp.sum(embed * embed, axis=1, keepdims=True) + 1e-06)
        exact = embed / length
        exact_ref[...] = exact
        unit_ref[...] = exact.astype(BF16)
        length_ref[...] = jnp.broadcast_to(length, length_ref.shape)

    samples, width = part.shape
    return call(
        body,
        None,
        [part, other],
        [((samples, width), F32), ((samples, width), BF16), ((samples, 128), F32)],
        6 * samples * width,
    )


def shares(rows):
    return 19 * rows // 128, 26 * rows // 128


def unit_rows(x):
    x = x.astype(F32)
    return (x / jnp.sqrt(jnp.sum(x * x, axis=1, keepdims=True) + 1e-06)).astype(BF16)


def normalize_sent(forward, direct):
    def body(a_ref, b_ref, f_ref, d_ref):
        f_ref[...] = unit_rows(a_ref[...])
        d_ref[...] = unit_rows(b_ref[...])

    return call(
        body,
        None,
        [forward, direct],
        [(forward.shape, BF16), (direct.shape, BF16)],
        8 * (forward.size + direct.size),
    )


def stage(place, hidden, weight, n_bank):
    samples, depth = hidden.shape
    pair = depth // 4 // n_bank * 2
    count = n_bank // 2 if pair % 256 == 0 else 0

    def body(place, hid_ref, w_hbm, o_ref, *refs):
        copy = pltpu.make_async_copy(w_hbm, o_ref, refs[-1])
        copy.start()
        for i, ref in enumerate(refs[:-1]):
            for g in range(4):
                start = pl.multiple_of(g * (depth // 4) + (place[2] ^ i) * pair, pair)
                ref[:, g * pair : (g + 1) * pair] = hid_ref[:, pl.ds(start, pair)]
        copy.wait()

    weight, *pieces = call(
        body,
        place,
        [hidden, weight],
        [(weight.shape, BF16)] + [((samples, 4 * pair), BF16)] * count,
        0,
        [pltpu.SemaphoreType.DMA(())],
        from_hbm=1,
    )
    return weight, pieces


def normalize(bank):
    rows, width = bank.shape
    steps = 8
    tile = rows // steps

    def body(x_hbm, o_ref, x_ref, sems):
        copies = [
            pltpu.make_async_copy(x_hbm.at[pl.ds(i * tile, tile)], x_ref.at[i], sems.at[i])
            for i in range(steps)
        ]
        for copy in copies:
            copy.start()
        for i in range(steps):
            copies[i].wait()
            o_ref[i * tile : (i + 1) * tile] = unit_rows(x_ref[i])

    return call(
        body,
        None,
        [bank],
        [(bank.shape, BF16)],
        8 * bank.size,
        [pltpu.VMEM((steps, tile, width), BF16), pltpu.SemaphoreType.DMA((steps,))],
        from_hbm=1,
    )[0]


def join(pieces):
    samples, width = pieces[0].shape
    count = len(pieces)

    def body(*refs):
        for i in range(count):
            refs[-1][i * samples : (i + 1) * samples] = refs[i][...]

    return call(body, None, pieces, [((count * samples, width), BF16)], 0)[0]


def bank_sums(line, blocks, before=None, samples=None):
    total, width = line.shape
    count = 1 if samples is None else total // samples

    def body(*refs):
        line_ref, rest = refs[0], refs[1:]
        row_refs, rest = rest[: len(blocks)], rest[len(blocks) :]
        outs, sums = rest[-1 - count : -1], rest[-1]
        started = before is not None
        if started:
            sums[...] = rest[0][...]
        for block, ref in zip(blocks, row_refs):
            tile = min(512, block.shape[0])
            for start in range(0, block.shape[0], tile):
                rows = ref[start : start + tile]
                scores = lax.dot_general(
                    line_ref[...], rows, (((1,), (1,)), ((), ())), preferred_element_type=F32
                )
                weight = jnp.exp(kernel_scale * scores).astype(BF16)
                term = jnp.dot(weight, rows, preferred_element_type=F32)
                sums[...] = sums[...] + term if started else term
                started = True
        for i, ref in enumerate(outs):
            size = total // count
            ref[...] = sums[i * size : (i + 1) * size].astype(ref.dtype)

    dims = (total // count, width)
    return call(
        body,
        None,
        [line] + list(blocks) + ([] if before is None else [before]),
        [(dims, BF16 if i else F32) for i in range(count)],
        4 * total * width * sum(block.shape[0] for block in blocks),
        [pltpu.VMEM((total, width), F32)],
    )


def pair_sums(unit, line, across):
    samples, width = unit.shape
    batch = 2 * line.shape[0]

    def body(unit_ref, line_ref, across_ref, out_ref):
        total = 0.0
        for ref, first in ((line_ref, True), (across_ref, False)):
            scores = lax.dot_general(
                unit_ref[...], ref[...], (((1,), (1,)), ((), ())), preferred_element_type=F32
            )
            weight = jnp.exp(kernel_scale * scores)
            if first:
                same = lax.broadcasted_iota(
                    jnp.int32, scores.shape, 0
                ) == lax.broadcasted_iota(jnp.int32, scores.shape, 1)
                weight = jnp.where(same, 0.0, weight)
            total = total + jnp.dot(
                weight.astype(BF16), ref[...], preferred_element_type=F32
            )
        out_ref[...] = total / (batch - 1)

    return call(
        body, None, [unit, line, across], [((samples, width), F32)], 4 * samples * width * batch
    )[0]


def embed_gradient(near, far, parts, exact, length, bank_rows):
    count = len(parts)

    def body(*refs):
        near_ref, far_ref, exact_ref, length_ref = refs[:4]
        total = far_ref[...]
        for ref in refs[4 : 4 + count]:
            total = total + ref[...].astype(F32)
        proof = near_ref[...] - total / bank_rows
        exact = exact_ref[...]
        radial = jnp.sum(exact * proof, axis=1, keepdims=True)
        refs[-1][...] = ((proof - exact * radial) / length_ref[:, :1]).astype(BF16)

    samples, width = near.shape
    return call(
        body,
        None,
        [near, far, exact, length] + list(parts),
        [((samples, width), BF16)],
        (count + 8) * samples * width,
    )[0]


def split_pairs(place, pieces):
    samples, width = pieces[0].shape
    block = width // 8
    count = len(pieces)

    def body(place, *refs):
        ins, outs = refs[:count], refs[count:]
        for out, y in zip(outs, (place[3], 1 - place[3])):
            for i, ref in enumerate(ins):
                for g in range(4):
                    start = pl.multiple_of((2 * g + y) * block, block)
                    out[i * samples : (i + 1) * samples, g * block : (g + 1) * block] = ref[
                        :, pl.ds(start, block)
                    ]

    return call(body, place, pieces, [((count * samples, 4 * block), BF16)] * 2, 0)


def turn(kept, given):
    rows, width = kept.shape

    def body(a_ref, b_ref, o_ref):
        o_ref[:, :rows] = a_ref[...].T
        o_ref[:, rows:] = b_ref[...].T

    return call(body, None, [kept, given], [((width, 2 * rows), BF16)], 0)[0]


def feature_sums(place, columns, grads, blocks):
    samples, width = grads[0].shape
    count = len(grads)
    piece = columns.shape[0] // 4
    batch = columns.shape[1]
    fresh = count > 1

    def body(place, cols_ref, *refs):
        ins, outs = refs[:count], refs[count:]
        held = outs[-1] if fresh else ins[0]
        if fresh:
            for i in range(count):
                held[i * samples : (i + 1) * samples] = ins[i][...]
        for ref, (side, core) in zip(outs, blocks):
            start = 2 * (place[0] ^ side) + (place[1] ^ core)
            start = pl.multiple_of(start * piece, piece)
            ref[...] = jnp.dot(
                cols_ref[pl.ds(start, piece), :], held[...], preferred_element_type=F32
            )

    return call(
        body,
        place,
        [columns] + list(grads),
        [((piece, width), F32)] * len(blocks) + [((batch, width), BF16)] * fresh,
        2 * len(blocks) * piece * width * batch,
    )


def add_round(a, b):
    def body(a_ref, b_ref, o_ref):
        o_ref[...] = (a_ref[...] + b_ref[...]).astype(BF16)

    return call(body, None, [a, b], [(a.shape, BF16)], a.size)[0]


def square_sums(kept, from_core, from_side, devices):
    rows, width = kept.shape

    def body(a_ref, b_ref, c_ref, grad_ref, out_ref):
        grad = a_ref[...] + b_ref[...] + c_ref[...].astype(F32)
        grad_ref[...] = grad
        squares = jnp.sum((grad * grad).reshape(rows // 8, 8, width), axis=0)
        tile = squares[:, :128]
        for i in range(1, width // 128):
            tile = tile + squares[:, i * 128 : (i + 1) * 128]
        tile = jnp.sum(tile, axis=0, keepdims=True)
        out_ref[...] = jnp.broadcast_to(tile[None], out_ref.shape)

    return call(
        body,
        None,
        [kept, from_core, from_side],
        [((rows, width), F32), ((devices, 1, 128), F32)],
        4 * rows * width,
    )


def scaled(gradient, squares, entries):
    rows = gradient.shape[0]
    steps = 4 if rows % 32 == 0 else 1
    size = rows // steps

    def body(g_ref, s_ref, o_hbm, held, sems):
        mean = jnp.sum(s_ref[...]) / entries
        factor = lax.rsqrt(jnp.full((1, 1), mean + 1e-06, F32))
        copies = []
        for i in range(steps):
            at = slice(i * size, (i + 1) * size)
            held[at] = g_ref[at] * factor
            copies.append(
                pltpu.make_async_copy(held.at[at], o_hbm.at[pl.ds(i * size, size)], sems.at[i])
            )
            copies[-1].start()
        for copy in copies:
            copy.wait()

    return call(
        body,
        None,
        [gradient, squares],
        [(gradient.shape, F32)],
        gradient.size,
        [pltpu.VMEM(gradient.shape, F32), pltpu.SemaphoreType.DMA((steps,))],
        to_hbm=True,
    )[0]


def by_feature(place, hidden, pieces, n_bank):
    samples, depth = hidden.shape
    piece = depth // 4 // n_bank
    if pieces:
        pieces = [swap(p, "bank", 2 * i) if i else p for i, p in enumerate(pieces)]
        kept, given = split_pairs(place, pieces)
        return turn(kept, swap(given, "bank", 1))
    pairs = hidden.reshape(samples, 4, n_bank // 2, 2 * piece)
    pieces = [
        lax.dynamic_index_in_dim(pairs, place[2] ^ i, 2, keepdims=False)
        for i in range(n_bank // 2)
    ]
    pieces = [swap(p, "bank", 2 * i) if i else p for i, p in enumerate(pieces)]
    columns = jnp.concatenate(pieces, 0)
    kept = lax.dynamic_slice_in_dim(columns, place[3] * piece, piece, 2)
    given = swap(lax.dynamic_slice_in_dim(columns, (1 - place[3]) * piece, piece, 2), "bank", 1)
    return jnp.concatenate([kept, given], 0).reshape(n_bank * samples, 4 * piece).T


def local(latents, shift, scale_mod, head_weight, bank):
    samples, depth = latents.shape
    width = head_weight.shape[1]
    n_gen = lax.axis_size("gen")
    n_bank = lax.axis_size("bank")
    gen = lax.axis_index("gen")
    me = lax.axis_index("bank")
    place = jnp.stack([gen // 2, gen % 2, me // 2, me % 2]).astype(jnp.int32)
    evens, odds = list(range(0, n_bank, 2)), list(range(1, n_bank, 2))

    head_other = swap(head_weight, "gen", 1)
    hidden, lent, own, forward, direct = modulate(place, latents, shift, scale_mod, bank)
    lent = swap(lent, "gen", 2)
    forward, direct = normalize_sent(forward, direct)
    head_weight, pieces = stage(place, hidden, head_weight, n_bank)
    bank_unit = normalize(bank)
    own_part = project(own, head_weight, head_other)
    returned = swap(project(lent, head_weight, head_other), "gen", 2)
    exact, unit, length = finish_embed(own_part, returned)

    columns = by_feature(place, hidden, pieces, n_bank)

    forward = swap(forward, "bank", 1)
    direct = swap(direct, "bank", 1)
    beside = swap(forward, "gen", 2)
    early = [forward, swap(forward, "gen", 1)]
    middle = [beside, direct]
    late = [swap(v, "gen", 1) for v in middle]

    line = [unit] + [swap(unit, "bank", m) for m in evens[1:]]
    line = join(line)
    across = swap(line, "bank", 1)
    sums = bank_sums(line, [bank_unit] + early)[0]
    sums = bank_sums(line, middle, sums)[0]
    far = bank_sums(line, late, sums, samples)
    parts = [swap(v, "bank", m) for m, v in zip(evens[1:], far[1:])]
    near = pair_sums(unit, line, across)
    grad_embed = embed_gradient(near, far[0], parts, exact, length, bank.shape[0] * n_bank)

    grads = {0: grad_embed}
    for m in range(n_bank - 2, 0, -1):
        grads[m] = swap(grad_embed, "bank", m)
    grads[n_bank - 1] = swap(grads[n_bank - 2], "bank", 1)
    grads = [grads[m] for m in evens + odds]
    for_core, grads = feature_sums(place, columns, grads, [(1, 1)])
    for_core = swap(for_core, "gen", 1)
    away, ours, home = feature_sums(place, columns, [grads], [(1, 0), (0, 0), (0, 1)])
    away = swap(add_round(away, for_core), "gen", 2)
    home = swap(home, "gen", 1)
    gradient, squares = square_sums(ours, home, away, n_gen * n_bank)
    squares = lax.all_to_all(squares, ("gen", "bank"), 0, 0, tiled=True)
    return scaled(gradient, squares, depth * width)


def solution(mesh):
    placed = (
        P(("gen", "bank"), None),
        P(("gen", "bank"), None),
        P(("gen", "bank"), None),
        P("gen", None),
        P("bank", None),
    )
    return jax.shard_map(
        lambda *args: local(*args),
        mesh=mesh,
        in_specs=placed,
        out_specs=P(("gen", "bank"), None),
        check_vma=False,
    )
```

```python
import jax
import jax.numpy as jnp
from jax import lax
from jax.experimental import pallas as pl
from jax.experimental.pallas import tpu as pltpu
from jax.sharding import PartitionSpec as P

kernel_scale = 32.0
F32, BF16 = jnp.float32, jnp.bfloat16
VMEM = pl.BlockSpec(memory_space=pltpu.VMEM)
HBM = pl.BlockSpec(memory_space=pltpu.HBM)


def swap(value, axis, mask):
    count = lax.axis_size(axis)
    return lax.ppermute(value, axis, [(i, i ^ mask) for i in range(count)])


def here():
    gen, bank = lax.axis_index("gen"), lax.axis_index("bank")
    return gen >> 1, gen & 1, bank >> 1, bank & 1


def call(body, arrays, outs, flops, scratch=(), to_hbm=False, from_hbm=0):
    far_away = [i >= len(arrays) - from_hbm for i in range(len(arrays))]
    arrays = [
        pltpu.with_memory_space_constraint(a, pltpu.HBM if there else pltpu.VMEM)
        for a, there in zip(arrays, far_away)
    ]
    make = jax.ShapeDtypeStruct if to_hbm else pltpu.VMEM
    size = sum(a.size * a.dtype.itemsize for a in arrays)
    return pl.pallas_call(
        body,
        in_specs=[HBM if there else VMEM for there in far_away],
        out_specs=[HBM if to_hbm else VMEM] * len(outs),
        out_shape=[make(dims, dtype) for dims, dtype in outs],
        scratch_shapes=list(scratch),
        compiler_params=pltpu.CompilerParams(vmem_limit_bytes=24 << 20),
        cost_estimate=pl.CostEstimate(flops=flops, bytes_accessed=size, transcendentals=0),
    )(*arrays)


def modulate(latents, shift, scale_mod, bank):
    samples, depth = latents.shape
    rows = 16
    quarter = depth // 4
    steps = samples // rows
    forward, direct = shares(bank.shape[0])

    def body(*refs):
        place = here()
        sources, bank_hbm = refs[:3], refs[3]
        hid_ref, lent_ref, own_ref, f_ref, d_ref = refs[4:9]
        held, sems, row_sems = refs[9:12], refs[12], refs[13]
        side, core = place[0], place[1]
        copies = [
            [
                pltpu.make_async_copy(src.at[pl.ds(r * rows, rows)], dst.at[r], sems.at[i, r])
                for i, (src, dst) in enumerate(zip(sources, held))
            ]
            for r in range(steps)
        ]
        starts = (2 * side + core) * forward, 4 * forward + core * direct
        sent = [
            pltpu.make_async_copy(
                bank_hbm.at[pl.ds(pl.multiple_of(start, 16), ref.shape[0])], ref, row_sems.at[i]
            )
            for i, (start, ref) in enumerate(zip(starts, (f_ref, d_ref)))
        ]
        for group in copies + [sent]:
            for copy in group:
                copy.start()
        for r in range(steps):
            for copy in copies[r]:
                copy.wait()
            at = slice(r * rows, (r + 1) * rows)
            x, b, s = (ref[r].astype(F32) for ref in held)
            inverse = lax.rsqrt(jnp.mean(x * x, axis=1, keepdims=True) + 1e-06)
            hid_ref[at] = (x * inverse * (1.0 + s) + b).astype(BF16)
        for ref, s in ((lent_ref, 1 - side), (own_ref, side)):
            for i, c in enumerate((core, 1 - core)):
                start = pl.multiple_of((2 * s + c) * quarter, quarter)
                ref[:, i * quarter : (i + 1) * quarter] = hid_ref[:, pl.ds(start, quarter)]
        for copy in sent:
            copy.wait()

    half = (samples, depth // 2)
    width = bank.shape[1]
    return call(
        body,
        [latents, shift, scale_mod, bank],
        [
            ((samples, depth), BF16),
            (half, BF16),
            (half, BF16),
            ((forward, width), BF16),
            ((direct, width), BF16),
        ],
        8 * samples * depth,
        [pltpu.VMEM((steps, rows, depth), BF16)] * 3
        + [pltpu.SemaphoreType.DMA((3, steps)), pltpu.SemaphoreType.DMA((2,))],
        from_hbm=4,
    )


def project(block, first, second):
    samples = block.shape[0]
    quarter, width = first.shape

    def body(x_ref, w_ref, v_ref, o_ref):
        o_ref[...] = jnp.dot(
            x_ref[:, :quarter], w_ref[...], preferred_element_type=F32
        ) + jnp.dot(x_ref[:, quarter:], v_ref[...], preferred_element_type=F32)

    return call(
        body, [block, first, second], [((samples, width), F32)], 4 * samples * quarter * width
    )[0]


def finish_embed(part, other):
    def body(a_ref, b_ref, exact_ref, unit_ref, length_ref):
        embed = a_ref[...] + b_ref[...].astype(F32)
        length = jnp.sqrt(jnp.sum(embed * embed, axis=1, keepdims=True) + 1e-06)
        exact = embed / length
        exact_ref[...] = exact
        unit_ref[...] = exact.astype(BF16)
        length_ref[...] = jnp.broadcast_to(length, length_ref.shape)

    samples, width = part.shape
    return call(
        body,
        [part, other],
        [((samples, width), F32), ((samples, width), BF16), ((samples, 128), F32)],
        6 * samples * width,
    )


def shares(rows):
    return 19 * rows // 128, 26 * rows // 128


def unit_rows(x):
    x = x.astype(F32)
    return (x / jnp.sqrt(jnp.sum(x * x, axis=1, keepdims=True) + 1e-06)).astype(BF16)


def normalize_sent(forward, direct):
    def body(a_ref, b_ref, f_ref, d_ref):
        f_ref[...] = unit_rows(a_ref[...])
        d_ref[...] = unit_rows(b_ref[...])

    return call(
        body,
        [forward, direct],
        [(forward.shape, BF16), (direct.shape, BF16)],
        8 * (forward.size + direct.size),
    )


def stage(hidden, weight, n_bank):
    samples, depth = hidden.shape
    pair = depth // 4 // n_bank * 2
    count = n_bank // 2 if pair % 256 == 0 else 0

    def body(hid_ref, w_hbm, o_ref, *refs):
        place = here()
        copy = pltpu.make_async_copy(w_hbm, o_ref, refs[-1])
        copy.start()
        for i, ref in enumerate(refs[:-1]):
            for g in range(4):
                start = pl.multiple_of(g * (depth // 4) + (place[2] ^ i) * pair, pair)
                ref[:, g * pair : (g + 1) * pair] = hid_ref[:, pl.ds(start, pair)]
        copy.wait()

    weight, *pieces = call(
        body,
        [hidden, weight],
        [(weight.shape, BF16)] + [((samples, 4 * pair), BF16)] * count,
        0,
        [pltpu.SemaphoreType.DMA(())],
        from_hbm=1,
    )
    return weight, pieces


def normalize(bank):
    rows, width = bank.shape
    steps = 8
    tile = rows // steps

    def body(x_hbm, o_ref, x_ref, sems):
        copies = [
            pltpu.make_async_copy(x_hbm.at[pl.ds(i * tile, tile)], x_ref.at[i], sems.at[i])
            for i in range(steps)
        ]
        for copy in copies:
            copy.start()
        for i in range(steps):
            copies[i].wait()
            o_ref[i * tile : (i + 1) * tile] = unit_rows(x_ref[i])

    return call(
        body,
        [bank],
        [(bank.shape, BF16)],
        8 * bank.size,
        [pltpu.VMEM((steps, tile, width), BF16), pltpu.SemaphoreType.DMA((steps,))],
        from_hbm=1,
    )[0]


def join(pieces):
    samples, width = pieces[0].shape
    count = len(pieces)

    def body(*refs):
        for i in range(count):
            refs[-1][i * samples : (i + 1) * samples] = refs[i][...]

    return call(body, pieces, [((count * samples, width), BF16)], 0)[0]


def bank_sums(line, blocks, before=None, samples=None):
    total, width = line.shape
    count = 1 if samples is None else total // samples

    def body(*refs):
        line_ref, rest = refs[0], refs[1:]
        row_refs, rest = rest[: len(blocks)], rest[len(blocks) :]
        held = None if before is None else rest[0]
        outs = rest[-count - (count > 1) :][:count]
        sums = rest[-1]
        for block, ref in zip(blocks, row_refs):
            tile = min(1024, block.shape[0])
            for start in range(0, block.shape[0], tile):
                rows = ref[start : start + tile]
                scores = lax.dot_general(
                    line_ref[...], rows, (((1,), (1,)), ((), ())), preferred_element_type=F32
                )
                weight = jnp.exp(kernel_scale * scores).astype(BF16)
                term = jnp.dot(weight, rows, preferred_element_type=F32)
                sums[...] = term if held is None else held[...] + term
                held = sums
        if count > 1:
            for i, ref in enumerate(outs):
                ref[...] = sums[i * samples : (i + 1) * samples].astype(ref.dtype)

    dims = (total // count, width)
    return call(
        body,
        [line] + list(blocks) + ([] if before is None else [before]),
        [(dims, BF16 if i else F32) for i in range(count)],
        4 * total * width * sum(block.shape[0] for block in blocks),
        [pltpu.VMEM((total, width), F32)] * (count > 1),
    )


def pair_sums(unit, line, across):
    samples, width = unit.shape
    batch = 2 * line.shape[0]

    def body(unit_ref, line_ref, across_ref, out_ref):
        total = 0.0
        for ref, first in ((line_ref, True), (across_ref, False)):
            scores = lax.dot_general(
                unit_ref[...], ref[...], (((1,), (1,)), ((), ())), preferred_element_type=F32
            )
            weight = jnp.exp(kernel_scale * scores)
            if first:
                same = lax.broadcasted_iota(
                    jnp.int32, scores.shape, 0
                ) == lax.broadcasted_iota(jnp.int32, scores.shape, 1)
                weight = jnp.where(same, 0.0, weight)
            total = total + jnp.dot(
                weight.astype(BF16), ref[...], preferred_element_type=F32
            )
        out_ref[...] = total / (batch - 1)

    return call(
        body, [unit, line, across], [((samples, width), F32)], 4 * samples * width * batch
    )[0]


def embed_gradient(near, far, parts, exact, length, bank_rows):
    count = len(parts)
    samples, width = near.shape
    half = width // 2

    def body(*refs):
        place = here()
        near_ref, far_ref, exact_ref, length_ref = refs[:4]
        keep_ref, give_ref = refs[-2:]
        total = far_ref[...]
        for ref in refs[4 : 4 + count]:
            total = total + ref[...].astype(F32)
        proof = near_ref[...] - total / bank_rows
        exact = exact_ref[...]
        radial = jnp.sum(exact * proof, axis=1, keepdims=True)
        grad = (proof - exact * radial) / length_ref[:, :1]
        first = place[0] == 0
        left, right = grad[:, :half], grad[:, half:]
        keep_ref[...] = jnp.where(first, left, right).astype(BF16)
        give_ref[...] = jnp.where(first, right, left).astype(BF16)

    return call(
        body,
        [near, far, exact, length] + list(parts),
        [((samples, half), BF16)] * 2,
        (count + 8) * samples * width,
    )


def split_pairs(pieces):
    samples, width = pieces[0].shape
    block = width // 8
    count = len(pieces)

    def body(*refs):
        place = here()
        ins, outs = refs[:count], refs[count:]
        for out, y in zip(outs, (place[3], 1 - place[3])):
            for i, ref in enumerate(ins):
                for g in range(4):
                    start = pl.multiple_of((2 * g + y) * block, block)
                    out[i * samples : (i + 1) * samples, g * block : (g + 1) * block] = ref[
                        :, pl.ds(start, block)
                    ]

    return call(body, pieces, [((count * samples, 4 * block), BF16)] * 2, 0)


def turn(kept, given):
    rows, width = kept.shape

    def body(a_ref, b_ref, o_ref):
        o_ref[:, :rows] = a_ref[...].T
        o_ref[:, rows:] = b_ref[...].T

    return call(body, [kept, given], [((width, 2 * rows), BF16)], 0)[0]


def feature_sums(columns, grads, core):
    fresh = len(grads) > 1
    arrays = [array for group in grads for array in group]
    samples = sum(array.shape[0] for array in grads[0]) // 2
    width = arrays[0].shape[1]
    batch = len(grads) * samples
    piece = columns[0].shape[0] // 4

    def body(own_ref, other_ref, *refs):
        place = here()
        outs = refs[len(arrays) :]
        held = outs[-1] if fresh else refs[0]
        if fresh:
            ins = iter(refs)
            for i, group in enumerate(grads):
                own = next(ins)
                if len(group) > 1:
                    own, other = own[...], next(ins)[...]
                else:
                    own, other = own[:samples], own[samples:]
                held[i * samples : (i + 1) * samples] = own
                held[batch + i * samples : batch + (i + 1) * samples] = other
        for side in (0, 1):
            start = 2 * (place[0] ^ side) + (place[1] ^ core)
            start = pl.multiple_of(start * piece, piece)
            outs[0][side * piece : (side + 1) * piece] = jnp.dot(
                own_ref[pl.ds(start, piece), :], held[:batch], preferred_element_type=F32
            ) + jnp.dot(
                other_ref[pl.ds(start, piece), :], held[batch:], preferred_element_type=F32
            )

    return call(
        body,
        list(columns) + arrays,
        [((2 * piece, width), F32)] + [((2 * batch, width), BF16)] * fresh,
        8 * piece * width * batch,
    )


def square_sums(kept, taken, devices):
    rows, width = kept.shape[0] // 2, kept.shape[1]

    def body(a_ref, b_ref, home_ref, away_ref, out_ref):
        total = 0.0
        for ref, at in ((home_ref, slice(0, rows)), (away_ref, slice(rows, 2 * rows))):
            block = a_ref[at] + b_ref[at]
            ref[...] = block
            total = total + jnp.sum((block * block).reshape(rows // 8, 8, width), axis=0)
        tile = total[:, :128]
        for i in range(1, width // 128):
            tile = tile + total[:, i * 128 : (i + 1) * 128]
        tile = jnp.sum(tile, axis=0, keepdims=True)
        out_ref[...] = jnp.broadcast_to(tile[None], out_ref.shape)

    return call(
        body,
        [kept, taken],
        [((rows, width), F32)] * 2 + [((devices, 1, 128), F32)],
        8 * rows * width,
    )


def scaled(home, other, squares, entries):
    rows, half = home.shape
    steps = 4 if rows % 32 == 0 else 1
    size = rows // steps

    def body(h_ref, a_ref, s_ref, o_hbm, held, sems):
        place = here()
        mean = jnp.sum(s_ref[...]) / entries
        factor = lax.rsqrt(jnp.full((1, 1), mean + 1e-06, F32))
        copies = []
        for i in range(steps):
            at = slice(i * size, (i + 1) * size)
            first = place[0] == 0
            held[at, :half] = jnp.where(first, h_ref[at], a_ref[at]) * factor
            held[at, half:] = jnp.where(first, a_ref[at], h_ref[at]) * factor
            copies.append(
                pltpu.make_async_copy(held.at[at], o_hbm.at[pl.ds(i * size, size)], sems.at[i])
            )
            copies[-1].start()
        for copy in copies:
            copy.wait()

    dims = (rows, 2 * half)
    return call(
        body,
        [home, other, squares],
        [(dims, F32)],
        2 * home.size,
        [pltpu.VMEM(dims, F32), pltpu.SemaphoreType.DMA((steps,))],
        to_hbm=True,
    )[0]


def by_feature(hidden, pieces, n_bank):
    samples, depth = hidden.shape
    piece = depth // 4 // n_bank
    if pieces:
        pieces = [swap(p, "bank", 2 * i) if i else p for i, p in enumerate(pieces)]
        kept, given = split_pairs(pieces)
        given = swap(given, "bank", 1)
        return turn(kept, given)
    place = here()
    pairs = hidden.reshape(samples, 4, n_bank // 2, 2 * piece)
    pieces = [
        lax.dynamic_index_in_dim(pairs, place[2] ^ i, 2, keepdims=False)
        for i in range(n_bank // 2)
    ]
    pieces = [swap(p, "bank", 2 * i) if i else p for i, p in enumerate(pieces)]
    columns = jnp.concatenate(pieces, 0)
    kept = lax.dynamic_slice_in_dim(columns, place[3] * piece, piece, 2)
    given = swap(lax.dynamic_slice_in_dim(columns, (1 - place[3]) * piece, piece, 2), "bank", 1)
    return jnp.concatenate([kept, given], 0).reshape(n_bank * samples, 4 * piece).T


def local(latents, shift, scale_mod, head_weight, bank):
    samples, depth = latents.shape
    width = head_weight.shape[1]
    n_gen = lax.axis_size("gen")
    n_bank = lax.axis_size("bank")
    evens, odds = list(range(0, n_bank, 2)), list(range(1, n_bank, 2))

    head_other = swap(head_weight, "gen", 1)
    hidden, lent, own, forward, direct = modulate(latents, shift, scale_mod, bank)
    lent = swap(lent, "gen", 2)
    forward, direct = normalize_sent(forward, direct)
    head_weight, pieces = stage(hidden, head_weight, n_bank)
    bank_unit = normalize(bank)
    own_part = project(own, head_weight, head_other)
    returned = swap(project(lent, head_weight, head_other), "gen", 2)
    exact, unit, length = finish_embed(own_part, returned)

    columns = by_feature(hidden, pieces, n_bank)

    forward = swap(forward, "bank", 1)
    direct = swap(direct, "bank", 1)
    beside = swap(forward, "gen", 2)
    early = [forward, swap(forward, "gen", 1)]
    middle = [beside, direct]
    late = [swap(v, "gen", 1) for v in middle]

    line = [unit] + [swap(unit, "bank", m) for m in evens[1:]]
    line = join(line)
    across = swap(line, "bank", 1)
    sums = bank_sums(line, [bank_unit] + early)[0]
    sums = bank_sums(line, middle, sums)[0]
    far = bank_sums(line, late, sums, samples)
    parts = [swap(v, "bank", m) for m, v in zip(evens[1:], far[1:])]
    near = pair_sums(unit, line, across)
    keep, give = embed_gradient(
        near, far[0], parts, exact, length, bank.shape[0] * n_bank
    )

    given = swap(give, "gen", 2)
    both = join([keep, given])
    high = range(n_bank - 2, n_bank // 2 - 1, -2)
    grads = {0: [keep, given]}
    for m in high:
        grads[m] = [swap(keep, "bank", m)]
    for m in high:
        grads[m].append(swap(given, "bank", m))
    for m in range(n_bank // 2 - 1, 0, -1):
        grads[m] = [swap(both, "bank", m)]
    for m in high:
        ahead = grads[m] if m == high[-1] else [join(grads[m])]
        grads[m + 1] = [swap(v, "bank", 1) for v in ahead]
    grads = [grads[m] for m in evens + odds]
    columns = [columns, swap(columns, "gen", 2)]
    for_core, grads = feature_sums(columns, grads, 1)
    taken = swap(for_core, "gen", 1)
    kept = feature_sums(columns, [[grads]], 0)[0]
    home, away, squares = square_sums(kept, taken, n_gen * n_bank)
    away = swap(away, "gen", 2)
    squares = lax.all_to_all(squares, ("gen", "bank"), 0, 0, tiled=True)
    return scaled(home, away, squares, depth * width)


def solution(mesh):
    placed = (
        P(("gen", "bank"), None),
        P(("gen", "bank"), None),
        P(("gen", "bank"), None),
        P("gen", None),
        P("bank", None),
    )
    return jax.shard_map(
        lambda *args: local(*args),
        mesh=mesh,
        in_specs=placed,
        out_specs=P(("gen", "bank"), None),
        check_vma=False,
    )
```

```python
import jax
import jax.numpy as jnp
from jax import lax
from jax.experimental import pallas as pl
from jax.experimental.pallas import tpu as pltpu
from jax.sharding import PartitionSpec as P

kernel_scale = 32.0
F32, BF16 = jnp.float32, jnp.bfloat16
GEN, BANK = "gen", "bank"
VMEM = pl.BlockSpec(memory_space=pltpu.VMEM)
HBM = pl.BlockSpec(memory_space=pltpu.HBM)


def swap(value, axis, mask):
    count = lax.axis_size(axis)
    return lax.ppermute(value, axis, [(i, i ^ mask) for i in range(count)])


def here():
    gen, bank = lax.axis_index(GEN), lax.axis_index(BANK)
    return gen >> 1, gen & 1, bank >> 1, bank & 1


def call(body, arrays, outs, flops, scratch=(), to_hbm=False, from_hbm=0):
    far_away = [i >= len(arrays) - from_hbm for i in range(len(arrays))]
    arrays = [
        pltpu.with_memory_space_constraint(a, pltpu.HBM if there else pltpu.VMEM)
        for a, there in zip(arrays, far_away)
    ]
    make = jax.ShapeDtypeStruct if to_hbm else pltpu.VMEM
    size = sum(a.size * a.dtype.itemsize for a in arrays)
    return pl.pallas_call(
        body,
        in_specs=[HBM if there else VMEM for there in far_away],
        out_specs=[HBM if to_hbm else VMEM] * len(outs),
        out_shape=[make(dims, dtype) for dims, dtype in outs],
        scratch_shapes=list(scratch),
        compiler_params=pltpu.CompilerParams(vmem_limit_bytes=24 << 20),
        cost_estimate=pl.CostEstimate(flops=flops, bytes_accessed=size, transcendentals=0),
    )(*arrays)


def modulate(latents, shift, scale_mod, bank):
    samples, depth = latents.shape
    rows = 16
    quarter = depth // 4
    steps = samples // rows
    forward, direct = shares(bank.shape[0])

    def body(*refs):
        place = here()
        sources, bank_hbm = refs[:3], refs[3]
        hid_ref, lent_ref, own_ref, f_ref, d_ref = refs[4:9]
        held, sems, row_sems = refs[9:12], refs[12], refs[13]
        side, core = place[0], place[1]
        copies = [
            [
                pltpu.make_async_copy(src.at[pl.ds(r * rows, rows)], dst.at[r], sems.at[i, r])
                for i, (src, dst) in enumerate(zip(sources, held))
            ]
            for r in range(steps)
        ]
        starts = (2 * side + core) * forward, 4 * forward + core * direct
        sent = [
            pltpu.make_async_copy(
                bank_hbm.at[pl.ds(pl.multiple_of(start, 16), ref.shape[0])], ref, row_sems.at[i]
            )
            for i, (start, ref) in enumerate(zip(starts, (f_ref, d_ref)))
        ]
        for group in copies + [sent]:
            for copy in group:
                copy.start()
        for r in range(steps):
            for copy in copies[r]:
                copy.wait()
            at = slice(r * rows, (r + 1) * rows)
            x, b, s = (ref[r].astype(F32) for ref in held)
            inverse = lax.rsqrt(jnp.mean(x * x, axis=1, keepdims=True) + 1e-06)
            hid_ref[at] = (x * inverse * (1.0 + s) + b).astype(BF16)
        for ref, s in ((lent_ref, 1 - side), (own_ref, side)):
            for i, c in enumerate((core, 1 - core)):
                start = pl.multiple_of((2 * s + c) * quarter, quarter)
                ref[:, i * quarter : (i + 1) * quarter] = hid_ref[:, pl.ds(start, quarter)]
        for copy in sent:
            copy.wait()

    half = (samples, depth // 2)
    width = bank.shape[1]
    return call(
        body,
        [latents, shift, scale_mod, bank],
        [
            ((samples, depth), BF16),
            (half, BF16),
            (half, BF16),
            ((forward, width), BF16),
            ((direct, width), BF16),
        ],
        8 * samples * depth,
        [pltpu.VMEM((steps, rows, depth), BF16)] * 3
        + [pltpu.SemaphoreType.DMA((3, steps)), pltpu.SemaphoreType.DMA((2,))],
        from_hbm=4,
    )


def project(lent, own, first, second):
    samples = own.shape[0]
    quarter, width = first.shape

    def body(x_ref, y_ref, w_ref, v_ref, lent_ref, own_ref, held):
        held[:samples] = x_ref[...]
        held[samples:] = y_ref[...]
        total = jnp.dot(
            held[:, :quarter], w_ref[...], preferred_element_type=F32
        ) + jnp.dot(held[:, quarter:], v_ref[...], preferred_element_type=F32)
        lent_ref[...] = total[:samples]
        own_ref[...] = total[samples:]

    return call(
        body,
        [lent, own, first, second],
        [((samples, width), F32)] * 2,
        8 * samples * quarter * width,
        [pltpu.VMEM((2 * samples, 2 * quarter), BF16)],
    )


def finish_embed(part, other):
    def body(a_ref, b_ref, exact_ref, unit_ref, length_ref):
        embed = a_ref[...] + b_ref[...].astype(F32)
        length = jnp.sqrt(jnp.sum(embed * embed, axis=1, keepdims=True) + 1e-06)
        exact = embed / length
        exact_ref[...] = exact
        unit_ref[...] = exact.astype(BF16)
        length_ref[...] = jnp.broadcast_to(length, length_ref.shape)

    samples, width = part.shape
    return call(
        body,
        [part, other],
        [((samples, width), F32), ((samples, width), BF16), ((samples, 128), F32)],
        6 * samples * width,
    )


def shares(rows):
    return 11 * rows // 64, 10 * rows // 64


def unit_rows(x):
    x = x.astype(F32)
    return (x / jnp.sqrt(jnp.sum(x * x, axis=1, keepdims=True) + 1e-06)).astype(BF16)


def normalize_sent(forward, direct):
    size = forward.shape[0] // 2
    width = forward.shape[1]

    def body(a_ref, b_ref, e_ref, f_ref, d_ref):
        e_ref[...] = unit_rows(a_ref[:size])
        f_ref[...] = unit_rows(a_ref[size:])
        d_ref[...] = unit_rows(b_ref[...])

    return call(
        body,
        [forward, direct],
        [((size, width), BF16)] * 2 + [(direct.shape, BF16)],
        8 * (forward.size + direct.size),
    )


def stage(hidden, weight, n_bank):
    samples, depth = hidden.shape
    pair = depth // 4 // n_bank * 2
    count = n_bank // 2 if pair % 256 == 0 else 0

    def body(hid_ref, w_hbm, o_ref, *refs):
        place = here()
        copy = pltpu.make_async_copy(w_hbm, o_ref, refs[-1])
        copy.start()
        for i, ref in enumerate(refs[:-1]):
            for g in range(4):
                start = pl.multiple_of(g * (depth // 4) + (place[2] ^ i) * pair, pair)
                ref[:, g * pair : (g + 1) * pair] = hid_ref[:, pl.ds(start, pair)]
        copy.wait()

    weight, *pieces = call(
        body,
        [hidden, weight],
        [(weight.shape, BF16)] + [((samples, 4 * pair), BF16)] * count,
        0,
        [pltpu.SemaphoreType.DMA(())],
        from_hbm=1,
    )
    return weight, pieces


def normalize(bank):
    rows, width = bank.shape
    steps = 8
    tile = rows // steps

    def body(x_hbm, o_ref, x_ref, sems):
        copies = [
            pltpu.make_async_copy(x_hbm.at[pl.ds(i * tile, tile)], x_ref.at[i], sems.at[i])
            for i in range(steps)
        ]
        for copy in copies:
            copy.start()
        for i in range(steps):
            copies[i].wait()
            o_ref[i * tile : (i + 1) * tile] = unit_rows(x_ref[i])

    return call(
        body,
        [bank],
        [(bank.shape, BF16)],
        8 * bank.size,
        [pltpu.VMEM((steps, tile, width), BF16), pltpu.SemaphoreType.DMA((steps,))],
        from_hbm=1,
    )[0]


def join(pieces):
    samples, width = pieces[0].shape
    count = len(pieces)

    def body(*refs):
        for i in range(count):
            refs[-1][i * samples : (i + 1) * samples] = refs[i][...]

    return call(body, pieces, [((count * samples, width), BF16)], 0)[0]


def bank_sums(line, blocks, before=None, samples=None):
    total, width = line.shape
    count = 1 if samples is None else total // samples

    def body(*refs):
        line_ref, rest = refs[0], refs[1:]
        row_refs, rest = rest[: len(blocks)], rest[len(blocks) :]
        held = None if before is None else rest[0]
        outs = rest[-count - (count > 1) :][:count]
        sums = rest[-1]
        for block, ref in zip(blocks, row_refs):
            tile = min(1024, block.shape[0])
            for start in range(0, block.shape[0], tile):
                rows = ref[start : start + tile]
                scores = lax.dot_general(
                    line_ref[...], rows, (((1,), (1,)), ((), ())), preferred_element_type=F32
                )
                weight = jnp.exp(kernel_scale * scores).astype(BF16)
                term = jnp.dot(weight, rows, preferred_element_type=F32)
                sums[...] = term if held is None else held[...] + term
                held = sums
        if count > 1:
            for i, ref in enumerate(outs):
                ref[...] = sums[i * samples : (i + 1) * samples].astype(ref.dtype)

    dims = (total // count, width)
    return call(
        body,
        [line] + list(blocks) + ([] if before is None else [before]),
        [(dims, BF16 if i else F32) for i in range(count)],
        4 * total * width * sum(block.shape[0] for block in blocks),
        [pltpu.VMEM((total, width), F32)] * (count > 1),
    )


def pair_sums(unit, line, across):
    samples, width = unit.shape
    batch = 2 * line.shape[0]

    def body(unit_ref, line_ref, across_ref, out_ref):
        total = 0.0
        for ref, first in ((line_ref, True), (across_ref, False)):
            scores = lax.dot_general(
                unit_ref[...], ref[...], (((1,), (1,)), ((), ())), preferred_element_type=F32
            )
            weight = jnp.exp(kernel_scale * scores)
            if first:
                same = lax.broadcasted_iota(
                    jnp.int32, scores.shape, 0
                ) == lax.broadcasted_iota(jnp.int32, scores.shape, 1)
                weight = jnp.where(same, 0.0, weight)
            total = total + jnp.dot(
                weight.astype(BF16), ref[...], preferred_element_type=F32
            )
        out_ref[...] = total / (batch - 1)

    return call(
        body,
        [unit, line, across],
        [((samples, width), F32)],
        4 * samples * width * batch,
    )[0]


def embed_gradient(near, far, parts, exact, length, bank_rows):
    count = len(parts)
    samples, width = near.shape
    half = width // 2

    def body(*refs):
        place = here()
        near_ref, far_ref, exact_ref, length_ref = refs[:4]
        keep_ref, give_ref = refs[-2:]
        total = far_ref[...]
        for ref in refs[4 : 4 + count]:
            total = total + ref[...].astype(F32)
        proof = near_ref[...] - total / bank_rows
        exact = exact_ref[...]
        radial = jnp.sum(exact * proof, axis=1, keepdims=True)
        grad = (proof - exact * radial) / length_ref[:, :1]
        first = place[0] == 0
        left, right = grad[:, :half], grad[:, half:]
        keep_ref[...] = jnp.where(first, left, right).astype(BF16)
        give_ref[...] = jnp.where(first, right, left).astype(BF16)

    return call(
        body,
        [near, far, exact, length] + list(parts),
        [((samples, half), BF16)] * 2,
        (count + 8) * samples * width,
    )


def split_pairs(pieces):
    samples, width = pieces[0].shape
    block = width // 8
    count = len(pieces)

    def body(*refs):
        place = here()
        ins, outs = refs[:count], refs[count:]
        for out, y in zip(outs, (place[3], 1 - place[3])):
            for i, ref in enumerate(ins):
                for g in range(4):
                    start = pl.multiple_of((2 * g + y) * block, block)
                    out[i * samples : (i + 1) * samples, g * block : (g + 1) * block] = ref[
                        :, pl.ds(start, block)
                    ]

    return call(
        body, pieces, [((count * samples, 4 * block), BF16)] * 2, 0
    )


def turn(kept, given):
    rows, width = kept.shape

    def body(a_ref, b_ref, o_ref):
        o_ref[:, :rows] = a_ref[...].T
        o_ref[:, rows:] = b_ref[...].T

    return call(body, [kept, given], [((width, 2 * rows), BF16)], 0)[0]


def feature_sums(columns, grads, core):
    fresh = len(grads) > 1
    arrays = [array for group in grads for array in group]
    samples = sum(array.shape[0] for array in grads[0]) // 2
    width = arrays[0].shape[1]
    batch = len(grads) * samples
    piece = columns[0].shape[0] // 4

    def body(own_ref, other_ref, *refs):
        place = here()
        outs = refs[len(arrays) :]
        held = outs[-1] if fresh else refs[0]
        if fresh:
            ins = iter(refs)
            for i, group in enumerate(grads):
                own = next(ins)
                if len(group) > 1:
                    own, other = own[...], next(ins)[...]
                else:
                    own, other = own[:samples], own[samples:]
                held[i * samples : (i + 1) * samples] = own
                held[batch + i * samples : batch + (i + 1) * samples] = other
        for side in (0, 1):
            start = 2 * (place[0] ^ side) + (place[1] ^ core)
            start = pl.multiple_of(start * piece, piece)
            outs[0][side * piece : (side + 1) * piece] = jnp.dot(
                own_ref[pl.ds(start, piece), :], held[:batch], preferred_element_type=F32
            ) + jnp.dot(
                other_ref[pl.ds(start, piece), :], held[batch:], preferred_element_type=F32
            )

    return call(
        body,
        list(columns) + arrays,
        [((2 * piece, width), F32)] + [((2 * batch, width), BF16)] * fresh,
        8 * piece * width * batch,
    )


def square_sums(kept, taken, devices):
    rows, width = kept.shape[0] // 2, kept.shape[1]

    def body(a_ref, b_ref, home_ref, away_ref, out_ref):
        total = 0.0
        for ref, at in ((home_ref, slice(0, rows)), (away_ref, slice(rows, 2 * rows))):
            block = a_ref[at] + b_ref[at]
            ref[...] = block
            total = total + jnp.sum((block * block).reshape(rows // 8, 8, width), axis=0)
        tile = total[:, :128]
        for i in range(1, width // 128):
            tile = tile + total[:, i * 128 : (i + 1) * 128]
        tile = jnp.sum(tile, axis=0, keepdims=True)
        out_ref[...] = jnp.broadcast_to(tile[None], out_ref.shape)

    return call(
        body,
        [kept, taken],
        [((rows, width), F32)] * 2 + [((devices, 1, 128), F32)],
        8 * rows * width,
    )


def scaled(home, other, squares, entries):
    rows, half = home.shape
    steps = 4 if rows % 32 == 0 else 1
    size = rows // steps

    def body(h_ref, a_ref, s_ref, o_hbm, held, sems):
        place = here()
        mean = jnp.sum(s_ref[...]) / entries
        factor = lax.rsqrt(jnp.full((1, 1), mean + 1e-06, F32))
        copies = []
        for i in range(steps):
            at = slice(i * size, (i + 1) * size)
            first = place[0] == 0
            held[at, :half] = jnp.where(first, h_ref[at], a_ref[at]) * factor
            held[at, half:] = jnp.where(first, a_ref[at], h_ref[at]) * factor
            copies.append(
                pltpu.make_async_copy(held.at[at], o_hbm.at[pl.ds(i * size, size)], sems.at[i])
            )
            copies[-1].start()
        for copy in copies:
            copy.wait()

    dims = (rows, 2 * half)
    return call(
        body,
        [home, other, squares],
        [(dims, F32)],
        2 * home.size,
        [pltpu.VMEM(dims, F32), pltpu.SemaphoreType.DMA((steps,))],
        to_hbm=True,
    )[0]


def by_feature(hidden, pieces, n_bank):
    samples, depth = hidden.shape
    piece = depth // 4 // n_bank
    if pieces:
        pieces = [swap(p, BANK, 2 * i) if i else p for i, p in enumerate(pieces)]
        kept, given = split_pairs(pieces)
        given = swap(given, BANK, 1)
        return turn(kept, given)
    place = here()
    pairs = hidden.reshape(samples, 4, n_bank // 2, 2 * piece)
    pieces = [
        lax.dynamic_index_in_dim(pairs, place[2] ^ i, 2, keepdims=False)
        for i in range(n_bank // 2)
    ]
    pieces = [swap(p, BANK, 2 * i) if i else p for i, p in enumerate(pieces)]
    columns = jnp.concatenate(pieces, 0)
    kept = lax.dynamic_slice_in_dim(columns, place[3] * piece, piece, 2)
    given = swap(lax.dynamic_slice_in_dim(columns, (1 - place[3]) * piece, piece, 2), BANK, 1)
    return jnp.concatenate([kept, given], 0).reshape(n_bank * samples, 4 * piece).T


def local(latents, shift, scale_mod, head_weight, bank):
    samples, depth = latents.shape
    width = head_weight.shape[1]
    n_gen = lax.axis_size(GEN)
    n_bank = lax.axis_size(BANK)
    evens, odds = list(range(0, n_bank, 2)), list(range(1, n_bank, 2))

    head_other = swap(head_weight, GEN, 1)
    hidden, lent, own, forward, direct = modulate(latents, shift, scale_mod, bank)
    lent = swap(lent, GEN, 2)
    *forward, direct = normalize_sent(forward, direct)
    head_weight, pieces = stage(hidden, head_weight, n_bank)
    bank_unit = normalize(bank)
    lent_part, own_part = project(lent, own, head_weight, head_other)
    returned = swap(lent_part, GEN, 2)
    exact, unit, length = finish_embed(own_part, returned)

    columns = by_feature(hidden, pieces, n_bank)

    forward = [swap(v, BANK, 1) for v in forward]
    direct = swap(direct, BANK, 1)
    beside = [swap(v, GEN, 2) for v in forward]
    forward, beside = join(forward), join(beside)
    early = [forward, swap(forward, GEN, 1)]
    middle = [beside, direct]
    late = [swap(v, GEN, 1) for v in middle]

    line = [unit] + [swap(unit, BANK, m) for m in evens[1:]]
    line = join(line)
    across = swap(line, BANK, 1)
    sums = bank_sums(line, [bank_unit] + early)[0]
    sums = bank_sums(line, middle, sums)[0]
    far = bank_sums(line, late, sums, samples)
    parts = [swap(v, BANK, m) for m, v in zip(evens[1:], far[1:])]
    near = pair_sums(unit, line, across)
    keep, give = embed_gradient(
        near, far[0], parts, exact, length, bank.shape[0] * n_bank
    )

    given = swap(give, GEN, 2)
    both = join([keep, given])
    high = range(n_bank - 2, n_bank // 2 - 1, -2)
    grads = {0: [keep, given]}
    for m in high:
        grads[m] = [swap(keep, BANK, m)]
    for m in high:
        grads[m].append(swap(given, BANK, m))
    for m in range(n_bank // 2 - 1, 0, -1):
        grads[m] = [swap(both, BANK, m)]
    for m in high:
        ahead = grads[m]
        grads[m + 1] = [swap(v, BANK, 1) for v in ahead]
    grads = [grads[m] for m in evens + odds]
    columns = [columns, swap(columns, GEN, 2)]
    for_core, grads = feature_sums(columns, grads, 1)
    taken = swap(for_core, GEN, 1)
    kept = feature_sums(columns, [[grads]], 0)[0]
    home, away, squares = square_sums(kept, taken, n_gen * n_bank)
    away = swap(away, GEN, 2)
    squares = lax.all_to_all(squares, (GEN, BANK), 0, 0, tiled=True)
    return scaled(home, away, squares, depth * width)


def solution(mesh):
    placed = (
        P((GEN, BANK), None),
        P((GEN, BANK), None),
        P((GEN, BANK), None),
        P(GEN, None),
        P(BANK, None),
    )
    return jax.shard_map(
        lambda *args: local(*args),
        mesh=mesh,
        in_specs=placed,
        out_specs=P((GEN, BANK), None),
        check_vma=False,
    )
```

```python
import jax
import jax.numpy as jnp
from jax import lax
from jax.experimental import pallas as pl
from jax.experimental.pallas import tpu as pltpu
from jax.sharding import PartitionSpec as P

kernel_scale = 32.0
F32, BF16 = jnp.float32, jnp.bfloat16
GEN, BANK = "gen", "bank"
VMEM = pl.BlockSpec(memory_space=pltpu.VMEM)
HBM = pl.BlockSpec(memory_space=pltpu.HBM)


def swap(value, axis, mask):
    count = lax.axis_size(axis)
    return lax.ppermute(value, axis, [(i, i ^ mask) for i in range(count)])


def here():
    gen, bank = lax.axis_index(GEN), lax.axis_index(BANK)
    return gen >> 1, gen & 1, bank >> 1, bank & 1


def call(body, arrays, outs, flops, scratch=(), to_hbm=False, from_hbm=0):
    far_away = [i >= len(arrays) - from_hbm for i in range(len(arrays))]
    arrays = [
        pltpu.with_memory_space_constraint(a, pltpu.HBM if there else pltpu.VMEM)
        for a, there in zip(arrays, far_away)
    ]
    make = jax.ShapeDtypeStruct if to_hbm else pltpu.VMEM
    size = sum(a.size * a.dtype.itemsize for a in arrays)
    return pl.pallas_call(
        body,
        in_specs=[HBM if there else VMEM for there in far_away],
        out_specs=[HBM if to_hbm else VMEM] * len(outs),
        out_shape=[make(dims, dtype) for dims, dtype in outs],
        scratch_shapes=list(scratch),
        compiler_params=pltpu.CompilerParams(vmem_limit_bytes=24 << 20),
        cost_estimate=pl.CostEstimate(flops=flops, bytes_accessed=size, transcendentals=0),
    )(*arrays)


def modulate(latents, shift, scale_mod, bank):
    samples, depth = latents.shape
    rows = 16
    quarter = depth // 4
    steps = samples // rows
    forward, direct = shares(bank.shape[0])

    def body(*refs):
        place = here()
        sources, bank_hbm = refs[:3], refs[3]
        hid_ref, lent_ref, own_ref, f_ref, d_ref = refs[4:9]
        held, sems, row_sems = refs[9:12], refs[12], refs[13]
        side, core = place[0], place[1]
        copies = [
            [
                pltpu.make_async_copy(src.at[pl.ds(r * rows, rows)], dst.at[r], sems.at[i, r])
                for i, (src, dst) in enumerate(zip(sources, held))
            ]
            for r in range(steps)
        ]
        starts = (2 * side + core) * forward, 4 * forward + core * direct
        sent = [
            pltpu.make_async_copy(
                bank_hbm.at[pl.ds(pl.multiple_of(start, 16), ref.shape[0])], ref, row_sems.at[i]
            )
            for i, (start, ref) in enumerate(zip(starts, (f_ref, d_ref)))
        ]
        for group in copies + [sent]:
            for copy in group:
                copy.start()
        for r in range(steps):
            for copy in copies[r]:
                copy.wait()
            at = slice(r * rows, (r + 1) * rows)
            x, b, s = (ref[r].astype(F32) for ref in held)
            inverse = lax.rsqrt(jnp.mean(x * x, axis=1, keepdims=True) + 1e-06)
            hid_ref[at] = (x * inverse * (1.0 + s) + b).astype(BF16)
        for ref, s in ((lent_ref, 1 - side), (own_ref, side)):
            for i, c in enumerate((core, 1 - core)):
                start = pl.multiple_of((2 * s + c) * quarter, quarter)
                ref[:, i * quarter : (i + 1) * quarter] = hid_ref[:, pl.ds(start, quarter)]
        for copy in sent:
            copy.wait()

    half = (samples, depth // 2)
    width = bank.shape[1]
    return call(
        body,
        [latents, shift, scale_mod, bank],
        [
            ((samples, depth), BF16),
            (half, BF16),
            (half, BF16),
            ((forward, width), BF16),
            ((direct, width), BF16),
        ],
        8 * samples * depth,
        [pltpu.VMEM((steps, rows, depth), BF16)] * 3
        + [pltpu.SemaphoreType.DMA((3, steps)), pltpu.SemaphoreType.DMA((2,))],
        from_hbm=4,
    )


def project(lent, own, first, second):
    samples = own.shape[0]
    quarter, width = first.shape

    def body(x_ref, y_ref, w_ref, v_ref, lent_ref, own_ref, held):
        held[:samples] = x_ref[...]
        held[samples:] = y_ref[...]
        total = jnp.dot(
            held[:, :quarter], w_ref[...], preferred_element_type=F32
        ) + jnp.dot(held[:, quarter:], v_ref[...], preferred_element_type=F32)
        lent_ref[...] = total[:samples]
        own_ref[...] = total[samples:]

    return call(
        body,
        [lent, own, first, second],
        [((samples, width), F32)] * 2,
        8 * samples * quarter * width,
        [pltpu.VMEM((2 * samples, 2 * quarter), BF16)],
    )


def finish_embed(part, other):
    def body(a_ref, b_ref, exact_ref, unit_ref, length_ref):
        embed = a_ref[...] + b_ref[...].astype(F32)
        length = jnp.sqrt(jnp.sum(embed * embed, axis=1, keepdims=True) + 1e-06)
        exact = embed / length
        exact_ref[...] = exact
        unit_ref[...] = exact.astype(BF16)
        length_ref[...] = jnp.broadcast_to(length, length_ref.shape)

    samples, width = part.shape
    return call(
        body,
        [part, other],
        [((samples, width), F32), ((samples, width), BF16), ((samples, 128), F32)],
        6 * samples * width,
    )


def shares(rows):
    return 11 * rows // 64, 10 * rows // 64


def unit_rows(x):
    x = x.astype(F32)
    return (x / jnp.sqrt(jnp.sum(x * x, axis=1, keepdims=True) + 1e-06)).astype(BF16)


def normalize_sent(forward, direct):
    size = forward.shape[0] // 2
    width = forward.shape[1]

    def body(a_ref, b_ref, e_ref, f_ref, d_ref):
        e_ref[...] = unit_rows(a_ref[:size])
        f_ref[...] = unit_rows(a_ref[size:])
        d_ref[...] = unit_rows(b_ref[...])

    return call(
        body,
        [forward, direct],
        [((size, width), BF16)] * 2 + [(direct.shape, BF16)],
        8 * (forward.size + direct.size),
    )


def stage(hidden, weight, n_bank):
    samples, depth = hidden.shape
    pair = depth // 4 // n_bank * 2
    count = n_bank // 2 if pair % 256 == 0 else 0

    def body(hid_ref, w_hbm, o_ref, *refs):
        place = here()
        copy = pltpu.make_async_copy(w_hbm, o_ref, refs[-1])
        copy.start()
        for i, ref in enumerate(refs[:-1]):
            for g in range(4):
                start = pl.multiple_of(g * (depth // 4) + (place[2] ^ i) * pair, pair)
                ref[:, g * pair : (g + 1) * pair] = hid_ref[:, pl.ds(start, pair)]
        copy.wait()

    weight, *pieces = call(
        body,
        [hidden, weight],
        [(weight.shape, BF16)] + [((samples, 4 * pair), BF16)] * count,
        0,
        [pltpu.SemaphoreType.DMA(())],
        from_hbm=1,
    )
    return weight, pieces


def normalize(bank):
    rows, width = bank.shape
    steps = 8
    tile = rows // steps

    def body(x_hbm, o_ref, x_ref, sems):
        copies = [
            pltpu.make_async_copy(x_hbm.at[pl.ds(i * tile, tile)], x_ref.at[i], sems.at[i])
            for i in range(steps)
        ]
        for copy in copies:
            copy.start()
        for i in range(steps):
            copies[i].wait()
            o_ref[i * tile : (i + 1) * tile] = unit_rows(x_ref[i])

    return call(
        body,
        [bank],
        [(bank.shape, BF16)],
        8 * bank.size,
        [pltpu.VMEM((steps, tile, width), BF16), pltpu.SemaphoreType.DMA((steps,))],
        from_hbm=1,
    )[0]


def join(pieces):
    samples, width = pieces[0].shape
    count = len(pieces)

    def body(*refs):
        for i in range(count):
            refs[-1][i * samples : (i + 1) * samples] = refs[i][...]

    return call(body, pieces, [((count * samples, width), BF16)], 0)[0]


def bank_sums(line, blocks, before=None, samples=None):
    total, width = line.shape
    count = 1 if samples is None else total // samples

    def body(*refs):
        line_ref, rest = refs[0], refs[1:]
        row_refs, rest = rest[: len(blocks)], rest[len(blocks) :]
        held = None if before is None else rest[0]
        outs = rest[-count - (count > 1) :][:count]
        sums = rest[-1]
        for block, ref in zip(blocks, row_refs):
            tile = min(1024, block.shape[0])
            for start in range(0, block.shape[0], tile):
                rows = ref[start : start + tile]
                scores = lax.dot_general(
                    line_ref[...], rows, (((1,), (1,)), ((), ())), preferred_element_type=F32
                )
                weight = jnp.exp(kernel_scale * scores).astype(BF16)
                term = jnp.dot(weight, rows, preferred_element_type=F32)
                sums[...] = term if held is None else held[...] + term
                held = sums
        if count > 1:
            for i, ref in enumerate(outs):
                ref[...] = sums[i * samples : (i + 1) * samples].astype(ref.dtype)

    dims = (total // count, width)
    return call(
        body,
        [line] + list(blocks) + ([] if before is None else [before]),
        [(dims, BF16 if i else F32) for i in range(count)],
        4 * total * width * sum(block.shape[0] for block in blocks),
        [pltpu.VMEM((total, width), F32)] * (count > 1),
    )


def pair_sums(unit, line, across):
    samples, width = unit.shape
    batch = 2 * line.shape[0]

    def body(unit_ref, line_ref, across_ref, out_ref):
        total = 0.0
        for ref, first in ((line_ref, True), (across_ref, False)):
            scores = lax.dot_general(
                unit_ref[...], ref[...], (((1,), (1,)), ((), ())), preferred_element_type=F32
            )
            weight = jnp.exp(kernel_scale * scores)
            if first:
                same = lax.broadcasted_iota(
                    jnp.int32, scores.shape, 0
                ) == lax.broadcasted_iota(jnp.int32, scores.shape, 1)
                weight = jnp.where(same, 0.0, weight)
            total = total + jnp.dot(
                weight.astype(BF16), ref[...], preferred_element_type=F32
            )
        out_ref[...] = total / (batch - 1)

    return call(
        body,
        [unit, line, across],
        [((samples, width), F32)],
        4 * samples * width * batch,
    )[0]


def embed_gradient(near, far, parts, exact, length, bank_rows):
    count = len(parts)
    samples, width = near.shape
    half = width // 2

    def body(*refs):
        place = here()
        near_ref, far_ref, exact_ref, length_ref = refs[:4]
        keep_ref, give_ref = refs[-2:]
        total = far_ref[...]
        for ref in refs[4 : 4 + count]:
            total = total + ref[...].astype(F32)
        proof = near_ref[...] - total / bank_rows
        exact = exact_ref[...]
        radial = jnp.sum(exact * proof, axis=1, keepdims=True)
        grad = (proof - exact * radial) / length_ref[:, :1]
        first = place[0] == 0
        left, right = grad[:, :half], grad[:, half:]
        keep_ref[...] = jnp.where(first, left, right).astype(BF16)
        give_ref[...] = jnp.where(first, right, left).astype(BF16)

    return call(
        body,
        [near, far, exact, length] + list(parts),
        [((samples, half), BF16)] * 2,
        (count + 8) * samples * width,
    )


def split_pairs(pieces):
    samples, width = pieces[0].shape
    block = width // 8
    count = len(pieces)

    def body(*refs):
        place = here()
        ins, outs = refs[:count], refs[count:]
        for out, y in zip(outs, (place[3], 1 - place[3])):
            for i, ref in enumerate(ins):
                for g in range(4):
                    start = pl.multiple_of((2 * g + y) * block, block)
                    out[i * samples : (i + 1) * samples, g * block : (g + 1) * block] = ref[
                        :, pl.ds(start, block)
                    ]

    return call(
        body, pieces, [((count * samples, 4 * block), BF16)] * 2, 0
    )


def turn(kept, given):
    rows, width = kept.shape

    def body(a_ref, b_ref, o_ref):
        o_ref[:, :rows] = a_ref[...].T
        o_ref[:, rows:] = b_ref[...].T

    return call(body, [kept, given], [((width, 2 * rows), BF16)], 0)[0]


def feature_sums(columns, grads, core):
    fresh = len(grads) > 1
    arrays = [array for group in grads for array in group]
    samples = sum(array.shape[0] for array in grads[0]) // 2
    width = arrays[0].shape[1]
    batch = len(grads) * samples
    piece = columns[0].shape[0] // 4

    def body(own_ref, other_ref, *refs):
        place = here()
        outs = refs[len(arrays) :]
        held = outs[-1] if fresh else refs[0]
        if fresh:
            ins = iter(refs)
            for i, group in enumerate(grads):
                own = next(ins)
                if len(group) > 1:
                    own, other = own[...], next(ins)[...]
                else:
                    own, other = own[:samples], own[samples:]
                held[i * samples : (i + 1) * samples] = own
                held[batch + i * samples : batch + (i + 1) * samples] = other
        for side in (0, 1):
            start = 2 * (place[0] ^ side) + (place[1] ^ core)
            start = pl.multiple_of(start * piece, piece)
            total = jnp.dot(
                own_ref[pl.ds(start, piece), :], held[:batch], preferred_element_type=F32
            ) + jnp.dot(
                other_ref[pl.ds(start, piece), :], held[batch:], preferred_element_type=F32
            )
            outs[0][side * piece : (side + 1) * piece] = total.astype(outs[0].dtype)

    return call(
        body,
        list(columns) + arrays,
        [((2 * piece, width), BF16 if core else F32)] + [((2 * batch, width), BF16)] * fresh,
        8 * piece * width * batch,
    )


def square_sums(kept, taken, devices):
    rows, width = kept.shape[0] // 2, kept.shape[1]

    def body(a_ref, b_ref, home_ref, away_ref, out_ref):
        total = 0.0
        for ref, at in ((home_ref, slice(0, rows)), (away_ref, slice(rows, 2 * rows))):
            block = a_ref[at] + b_ref[at].astype(F32)
            ref[...] = block
            total = total + jnp.sum((block * block).reshape(rows // 8, 8, width), axis=0)
        tile = total[:, :128]
        for i in range(1, width // 128):
            tile = tile + total[:, i * 128 : (i + 1) * 128]
        tile = jnp.sum(tile, axis=0, keepdims=True)
        out_ref[...] = jnp.broadcast_to(tile[None], out_ref.shape)

    return call(
        body,
        [kept, taken],
        [((rows, width), F32)] * 2 + [((devices, 1, 128), F32)],
        8 * rows * width,
    )


def scaled(home, other, squares, entries):
    rows, half = home.shape
    steps = 4 if rows % 32 == 0 else 1
    size = rows // steps

    def body(h_ref, a_ref, s_ref, o_hbm, held, sems):
        place = here()
        mean = jnp.sum(s_ref[...]) / entries
        factor = lax.rsqrt(jnp.full((1, 1), mean + 1e-06, F32))
        copies = []
        for i in range(steps):
            at = slice(i * size, (i + 1) * size)
            first = place[0] == 0
            held[at, :half] = jnp.where(first, h_ref[at], a_ref[at]) * factor
            held[at, half:] = jnp.where(first, a_ref[at], h_ref[at]) * factor
            copies.append(
                pltpu.make_async_copy(held.at[at], o_hbm.at[pl.ds(i * size, size)], sems.at[i])
            )
            copies[-1].start()
        for copy in copies:
            copy.wait()

    dims = (rows, 2 * half)
    return call(
        body,
        [home, other, squares],
        [(dims, F32)],
        2 * home.size,
        [pltpu.VMEM(dims, F32), pltpu.SemaphoreType.DMA((steps,))],
        to_hbm=True,
    )[0]


def by_feature(hidden, pieces, n_bank):
    samples, depth = hidden.shape
    piece = depth // 4 // n_bank
    if pieces:
        pieces = [swap(p, BANK, 2 * i) if i else p for i, p in enumerate(pieces)]
        kept, given = split_pairs(pieces)
        given = swap(given, BANK, 1)
        return turn(kept, given)
    place = here()
    pairs = hidden.reshape(samples, 4, n_bank // 2, 2 * piece)
    pieces = [
        lax.dynamic_index_in_dim(pairs, place[2] ^ i, 2, keepdims=False)
        for i in range(n_bank // 2)
    ]
    pieces = [swap(p, BANK, 2 * i) if i else p for i, p in enumerate(pieces)]
    columns = jnp.concatenate(pieces, 0)
    kept = lax.dynamic_slice_in_dim(columns, place[3] * piece, piece, 2)
    given = swap(lax.dynamic_slice_in_dim(columns, (1 - place[3]) * piece, piece, 2), BANK, 1)
    return jnp.concatenate([kept, given], 0).reshape(n_bank * samples, 4 * piece).T


def local(latents, shift, scale_mod, head_weight, bank):
    samples, depth = latents.shape
    width = head_weight.shape[1]
    n_gen = lax.axis_size(GEN)
    n_bank = lax.axis_size(BANK)
    evens, odds = list(range(0, n_bank, 2)), list(range(1, n_bank, 2))

    head_other = swap(head_weight, GEN, 1)
    hidden, lent, own, forward, direct = modulate(latents, shift, scale_mod, bank)
    lent = swap(lent, GEN, 2)
    *forward, direct = normalize_sent(forward, direct)
    head_weight, pieces = stage(hidden, head_weight, n_bank)
    bank_unit = normalize(bank)
    lent_part, own_part = project(lent, own, head_weight, head_other)
    returned = swap(lent_part, GEN, 2)
    exact, unit, length = finish_embed(own_part, returned)

    columns = by_feature(hidden, pieces, n_bank)

    forward = [swap(v, BANK, 1) for v in forward]
    direct = swap(direct, BANK, 1)
    beside = [swap(v, GEN, 2) for v in forward]
    forward, beside = join(forward), join(beside)
    early = [forward, swap(forward, GEN, 1)]
    middle = [beside, direct]
    late = [swap(v, GEN, 1) for v in middle]

    line = [unit] + [swap(unit, BANK, m) for m in evens[1:]]
    line = join(line)
    across = swap(line, BANK, 1)
    sums = bank_sums(line, [bank_unit] + early)[0]
    sums = bank_sums(line, middle, sums)[0]
    far = bank_sums(line, late, sums, samples)
    parts = [swap(v, BANK, m) for m, v in zip(evens[1:], far[1:])]
    near = pair_sums(unit, line, across)
    keep, give = embed_gradient(
        near, far[0], parts, exact, length, bank.shape[0] * n_bank
    )

    given = swap(give, GEN, 2)
    both = join([keep, given])
    high = range(n_bank - 2, n_bank // 2 - 1, -2)
    grads = {0: [keep, given]}
    for m in high:
        grads[m] = [swap(keep, BANK, m)]
    for m in high:
        grads[m].append(swap(given, BANK, m))
    for m in range(n_bank // 2 - 1, 0, -1):
        grads[m] = [swap(both, BANK, m)]
    for m in high:
        ahead = grads[m]
        grads[m + 1] = [swap(v, BANK, 1) for v in ahead]
    grads = [grads[m] for m in evens + odds]
    columns = [columns, swap(columns, GEN, 2)]
    for_core, grads = feature_sums(columns, grads, 1)
    taken = swap(for_core, GEN, 1)
    kept = feature_sums(columns, [[grads]], 0)[0]
    home, away, squares = square_sums(kept, taken, n_gen * n_bank)
    away = swap(away, GEN, 2)
    squares = lax.all_to_all(squares, (GEN, BANK), 0, 0, tiled=True)
    return scaled(home, away, squares, depth * width)


def solution(mesh):
    placed = (
        P((GEN, BANK), None),
        P((GEN, BANK), None),
        P((GEN, BANK), None),
        P(GEN, None),
        P(BANK, None),
    )
    return jax.shard_map(
        lambda *args: local(*args),
        mesh=mesh,
        in_specs=placed,
        out_specs=P((GEN, BANK), None),
        check_vma=False,
    )
```

```python
import jax
import jax.numpy as jnp
from jax import lax
from jax.experimental import pallas as pl
from jax.experimental.pallas import tpu as pltpu
from jax.sharding import PartitionSpec as P

kernel_scale = 32.0
F32, BF16 = jnp.float32, jnp.bfloat16
GEN, BANK = "gen", "bank"
VMEM = pl.BlockSpec(memory_space=pltpu.VMEM)
HBM = pl.BlockSpec(memory_space=pltpu.HBM)


def swap(value, axis, mask):
    count = lax.axis_size(axis)
    return lax.ppermute(value, axis, [(i, i ^ mask) for i in range(count)])


def here():
    gen, bank = lax.axis_index(GEN), lax.axis_index(BANK)
    return gen >> 1, gen & 1, bank >> 1, bank & 1


def call(body, arrays, outs, flops, scratch=(), to_hbm=False, from_hbm=0):
    far_away = [i >= len(arrays) - from_hbm for i in range(len(arrays))]
    arrays = [
        pltpu.with_memory_space_constraint(a, pltpu.HBM if there else pltpu.VMEM)
        for a, there in zip(arrays, far_away)
    ]
    make = jax.ShapeDtypeStruct if to_hbm else pltpu.VMEM
    size = sum(a.size * a.dtype.itemsize for a in arrays)
    return pl.pallas_call(
        body,
        in_specs=[HBM if there else VMEM for there in far_away],
        out_specs=[HBM if to_hbm else VMEM] * len(outs),
        out_shape=[make(dims, dtype) for dims, dtype in outs],
        scratch_shapes=list(scratch),
        compiler_params=pltpu.CompilerParams(vmem_limit_bytes=24 << 20),
        cost_estimate=pl.CostEstimate(flops=flops, bytes_accessed=size, transcendentals=0),
    )(*arrays)


def modulate(latents, shift, scale_mod, bank):
    samples, depth = latents.shape
    rows = 16
    quarter = depth // 4
    steps = samples // rows
    forward, direct = shares(bank.shape[0])

    def body(*refs):
        place = here()
        sources, bank_hbm = refs[:3], refs[3]
        hid_ref, lent_ref, own_ref, f_ref, d_ref = refs[4:9]
        held, sems, row_sems = refs[9:12], refs[12], refs[13]
        side, core = place[0], place[1]
        copies = [
            [
                pltpu.make_async_copy(src.at[pl.ds(r * rows, rows)], dst.at[r], sems.at[i, r])
                for i, (src, dst) in enumerate(zip(sources, held))
            ]
            for r in range(steps)
        ]
        starts = (2 * side + core) * forward, 4 * forward + core * direct
        sent = [
            pltpu.make_async_copy(
                bank_hbm.at[pl.ds(pl.multiple_of(start, 16), ref.shape[0])], ref, row_sems.at[i]
            )
            for i, (start, ref) in enumerate(zip(starts, (f_ref, d_ref)))
        ]
        for group in copies + [sent]:
            for copy in group:
                copy.start()
        for r in range(steps):
            for copy in copies[r]:
                copy.wait()
            at = slice(r * rows, (r + 1) * rows)
            x, b, s = (ref[r].astype(F32) for ref in held)
            inverse = lax.rsqrt(jnp.mean(x * x, axis=1, keepdims=True) + 1e-06)
            hid_ref[at] = (x * inverse * (1.0 + s) + b).astype(BF16)
        for ref, s in ((lent_ref, 1 - side), (own_ref, side)):
            for i, c in enumerate((core, 1 - core)):
                start = pl.multiple_of((2 * s + c) * quarter, quarter)
                ref[:, i * quarter : (i + 1) * quarter] = hid_ref[:, pl.ds(start, quarter)]
        for copy in sent:
            copy.wait()

    half = (samples, depth // 2)
    width = bank.shape[1]
    return call(
        body,
        [latents, shift, scale_mod, bank],
        [
            ((samples, depth), BF16),
            (half, BF16),
            (half, BF16),
            ((forward, width), BF16),
            ((direct, width), BF16),
        ],
        8 * samples * depth,
        [pltpu.VMEM((steps, rows, depth), BF16)] * 3
        + [pltpu.SemaphoreType.DMA((3, steps)), pltpu.SemaphoreType.DMA((2,))],
        from_hbm=4,
    )


def project(lent, own, first, second):
    samples = own.shape[0]
    quarter, width = first.shape

    def body(x_ref, y_ref, w_ref, v_ref, lent_ref, own_ref, held):
        held[:samples] = x_ref[...]
        held[samples:] = y_ref[...]
        total = jnp.dot(
            held[:, :quarter], w_ref[...], preferred_element_type=F32
        ) + jnp.dot(held[:, quarter:], v_ref[...], preferred_element_type=F32)
        lent_ref[...] = total[:samples]
        own_ref[...] = total[samples:]

    return call(
        body,
        [lent, own, first, second],
        [((samples, width), F32)] * 2,
        8 * samples * quarter * width,
        [pltpu.VMEM((2 * samples, 2 * quarter), BF16)],
    )


def finish_embed(part, other):
    def body(a_ref, b_ref, exact_ref, unit_ref, length_ref):
        embed = a_ref[...] + b_ref[...].astype(F32)
        length = jnp.sqrt(jnp.sum(embed * embed, axis=1, keepdims=True) + 1e-06)
        exact = embed / length
        exact_ref[...] = exact
        unit_ref[...] = exact.astype(BF16)
        length_ref[...] = jnp.broadcast_to(length, length_ref.shape)

    samples, width = part.shape
    return call(
        body,
        [part, other],
        [((samples, width), F32), ((samples, width), BF16), ((samples, 128), F32)],
        6 * samples * width,
    )


def shares(rows):
    return 11 * rows // 64, 10 * rows // 64


def unit_rows(x):
    x = x.astype(F32)
    return (x / jnp.sqrt(jnp.sum(x * x, axis=1, keepdims=True) + 1e-06)).astype(BF16)


def normalize_sent(forward, direct):
    size = forward.shape[0] // 2
    width = forward.shape[1]

    def body(a_ref, b_ref, e_ref, f_ref, d_ref):
        e_ref[...] = unit_rows(a_ref[:size])
        f_ref[...] = unit_rows(a_ref[size:])
        d_ref[...] = unit_rows(b_ref[...])

    return call(
        body,
        [forward, direct],
        [((size, width), BF16)] * 2 + [(direct.shape, BF16)],
        8 * (forward.size + direct.size),
    )


def stage(hidden, weight, n_bank):
    samples, depth = hidden.shape
    pair = depth // 4 // n_bank * 2
    count = n_bank // 2 if pair % 256 == 0 else 0

    def body(hid_ref, w_hbm, o_ref, *refs):
        place = here()
        copy = pltpu.make_async_copy(w_hbm, o_ref, refs[-1])
        copy.start()
        for i, ref in enumerate(refs[:-1]):
            for g in range(4):
                start = pl.multiple_of(g * (depth // 4) + (place[2] ^ i) * pair, pair)
                ref[:, g * pair : (g + 1) * pair] = hid_ref[:, pl.ds(start, pair)]
        copy.wait()

    weight, *pieces = call(
        body,
        [hidden, weight],
        [(weight.shape, BF16)] + [((samples, 4 * pair), BF16)] * count,
        0,
        [pltpu.SemaphoreType.DMA(())],
        from_hbm=1,
    )
    return weight, pieces


def normalize(bank):
    rows, width = bank.shape
    steps = 8
    tile = rows // steps

    def body(x_hbm, o_ref, x_ref, sems):
        copies = [
            pltpu.make_async_copy(x_hbm.at[pl.ds(i * tile, tile)], x_ref.at[i], sems.at[i])
            for i in range(steps)
        ]
        for copy in copies:
            copy.start()
        for i in range(steps):
            copies[i].wait()
            o_ref[i * tile : (i + 1) * tile] = unit_rows(x_ref[i])

    return call(
        body,
        [bank],
        [(bank.shape, BF16)],
        8 * bank.size,
        [pltpu.VMEM((steps, tile, width), BF16), pltpu.SemaphoreType.DMA((steps,))],
        from_hbm=1,
    )[0]


def join(pieces):
    width = pieces[0].shape[1]
    heights = [piece.shape[0] for piece in pieces]

    def body(*refs):
        start = 0
        for ref, height in zip(refs, heights):
            refs[-1][start : start + height] = ref[...]
            start += height

    return call(body, pieces, [((sum(heights), width), BF16)], 0)[0]


def bank_sums(line, blocks, before=None, samples=None):
    total, width = line.shape
    count = 1 if samples is None else total // samples

    def body(*refs):
        line_ref, rest = refs[0], refs[1:]
        row_refs, rest = rest[: len(blocks)], rest[len(blocks) :]
        held = None if before is None else rest[0]
        outs = rest[-count - (count > 1) :][:count]
        sums = rest[-1]
        for block, ref in zip(blocks, row_refs):
            tile = min(1024, block.shape[0])
            for start in range(0, block.shape[0], tile):
                rows = ref[start : start + tile]
                scores = lax.dot_general(
                    line_ref[...], rows, (((1,), (1,)), ((), ())), preferred_element_type=F32
                )
                weight = jnp.exp(kernel_scale * scores).astype(BF16)
                term = jnp.dot(weight, rows, preferred_element_type=F32)
                sums[...] = term if held is None else held[...] + term
                held = sums
        if count > 1:
            for i, ref in enumerate(outs):
                ref[...] = sums[i * samples : (i + 1) * samples].astype(ref.dtype)

    dims = (total // count, width)
    return call(
        body,
        [line] + list(blocks) + ([] if before is None else [before]),
        [(dims, BF16 if i else F32) for i in range(count)],
        4 * total * width * sum(block.shape[0] for block in blocks),
        [pltpu.VMEM((total, width), F32)] * (count > 1),
    )


def pair_sums(unit, line, across):
    samples, width = unit.shape
    batch = 2 * line.shape[0]

    def body(unit_ref, line_ref, across_ref, out_ref):
        total = 0.0
        for ref, first in ((line_ref, True), (across_ref, False)):
            scores = lax.dot_general(
                unit_ref[...], ref[...], (((1,), (1,)), ((), ())), preferred_element_type=F32
            )
            weight = jnp.exp(kernel_scale * scores)
            if first:
                same = lax.broadcasted_iota(
                    jnp.int32, scores.shape, 0
                ) == lax.broadcasted_iota(jnp.int32, scores.shape, 1)
                weight = jnp.where(same, 0.0, weight)
            total = total + jnp.dot(
                weight.astype(BF16), ref[...], preferred_element_type=F32
            )
        out_ref[...] = total / (batch - 1)

    return call(
        body,
        [unit, line, across],
        [((samples, width), F32)],
        4 * samples * width * batch,
    )[0]


def embed_gradient(near, far, parts, exact, length, bank_rows):
    count = len(parts)
    samples, width = near.shape
    half = width // 2

    def body(*refs):
        place = here()
        near_ref, far_ref, exact_ref, length_ref = refs[:4]
        keep_ref, give_ref = refs[-2:]
        total = far_ref[...]
        for ref in refs[4 : 4 + count]:
            total = total + ref[...].astype(F32)
        proof = near_ref[...] - total / bank_rows
        exact = exact_ref[...]
        radial = jnp.sum(exact * proof, axis=1, keepdims=True)
        grad = (proof - exact * radial) / length_ref[:, :1]
        first = place[0] == 0
        left, right = grad[:, :half], grad[:, half:]
        keep_ref[...] = jnp.where(first, left, right).astype(BF16)
        give_ref[...] = jnp.where(first, right, left).astype(BF16)

    return call(
        body,
        [near, far, exact, length] + list(parts),
        [((samples, half), BF16)] * 2,
        (count + 8) * samples * width,
    )


def split_pairs(pieces):
    samples, width = pieces[0].shape
    block = width // 8
    count = len(pieces)

    def body(*refs):
        place = here()
        ins, outs = refs[:count], refs[count:]
        for out, y in zip(outs, (place[3], 1 - place[3])):
            for i, ref in enumerate(ins):
                for g in range(4):
                    start = pl.multiple_of((2 * g + y) * block, block)
                    out[i * samples : (i + 1) * samples, g * block : (g + 1) * block] = ref[
                        :, pl.ds(start, block)
                    ]

    return call(
        body, pieces, [((count * samples, 4 * block), BF16)] * 2, 0
    )


def turn(kept, given):
    rows, width = kept.shape

    def body(a_ref, b_ref, o_ref):
        o_ref[:, :rows] = a_ref[...].T
        o_ref[:, rows:] = b_ref[...].T

    return call(body, [kept, given], [((width, 2 * rows), BF16)], 0)[0]


def feature_sums(columns, grads, core):
    fresh = len(grads) > 1
    arrays = [array for group in grads for array in group]
    samples = sum(array.shape[0] for array in grads[0]) // 2
    width = arrays[0].shape[1]
    batch = len(grads) * samples
    piece = columns[0].shape[0] // 4

    def body(own_ref, other_ref, *refs):
        place = here()
        outs = refs[len(arrays) :]
        held = outs[-1] if fresh else refs[0]
        if fresh:
            ins = iter(refs)
            for i, group in enumerate(grads):
                own = next(ins)
                if len(group) > 1:
                    own, other = own[...], next(ins)[...]
                else:
                    own, other = own[:samples], own[samples:]
                held[i * samples : (i + 1) * samples] = own
                held[batch + i * samples : batch + (i + 1) * samples] = other
        for side in (0, 1):
            start = 2 * (place[0] ^ side) + (place[1] ^ core)
            start = pl.multiple_of(start * piece, piece)
            total = jnp.dot(
                own_ref[pl.ds(start, piece), :], held[:batch], preferred_element_type=F32
            ) + jnp.dot(
                other_ref[pl.ds(start, piece), :], held[batch:], preferred_element_type=F32
            )
            outs[0][side * piece : (side + 1) * piece] = total.astype(outs[0].dtype)

    return call(
        body,
        list(columns) + arrays,
        [((2 * piece, width), BF16 if core else F32)] + [((2 * batch, width), BF16)] * fresh,
        8 * piece * width * batch,
    )


def square_sums(kept, taken, devices):
    rows, width = kept.shape[0] // 2, kept.shape[1]

    def body(a_ref, b_ref, home_ref, away_ref, out_ref):
        total = 0.0
        for ref, at in ((home_ref, slice(0, rows)), (away_ref, slice(rows, 2 * rows))):
            block = a_ref[at] + b_ref[at].astype(F32)
            ref[...] = block
            total = total + jnp.sum((block * block).reshape(rows // 8, 8, width), axis=0)
        tile = total[:, :128]
        for i in range(1, width // 128):
            tile = tile + total[:, i * 128 : (i + 1) * 128]
        tile = jnp.sum(tile, axis=0, keepdims=True)
        out_ref[...] = jnp.broadcast_to(tile[None], out_ref.shape)

    return call(
        body,
        [kept, taken],
        [((rows, width), F32)] * 2 + [((devices, 1, 128), F32)],
        8 * rows * width,
    )


def scaled(home, other, squares, entries):
    rows, half = home.shape
    steps = 4 if rows % 32 == 0 else 1
    size = rows // steps

    def body(h_ref, a_ref, s_ref, o_hbm, held, sems):
        place = here()
        mean = jnp.sum(s_ref[...]) / entries
        factor = lax.rsqrt(jnp.full((1, 1), mean + 1e-06, F32))
        copies = []
        for i in range(steps):
            at = slice(i * size, (i + 1) * size)
            first = place[0] == 0
            held[at, :half] = jnp.where(first, h_ref[at], a_ref[at]) * factor
            held[at, half:] = jnp.where(first, a_ref[at], h_ref[at]) * factor
            copies.append(
                pltpu.make_async_copy(held.at[at], o_hbm.at[pl.ds(i * size, size)], sems.at[i])
            )
            copies[-1].start()
        for copy in copies:
            copy.wait()

    dims = (rows, 2 * half)
    return call(
        body,
        [home, other, squares],
        [(dims, F32)],
        2 * home.size,
        [pltpu.VMEM(dims, F32), pltpu.SemaphoreType.DMA((steps,))],
        to_hbm=True,
    )[0]


def by_feature(hidden, pieces, n_bank):
    samples, depth = hidden.shape
    piece = depth // 4 // n_bank
    if pieces:
        pieces = [swap(p, BANK, 2 * i) if i else p for i, p in enumerate(pieces)]
        kept, given = split_pairs(pieces)
        given = swap(given, BANK, 1)
        return turn(kept, given)
    place = here()
    pairs = hidden.reshape(samples, 4, n_bank // 2, 2 * piece)
    pieces = [
        lax.dynamic_index_in_dim(pairs, place[2] ^ i, 2, keepdims=False)
        for i in range(n_bank // 2)
    ]
    pieces = [swap(p, BANK, 2 * i) if i else p for i, p in enumerate(pieces)]
    columns = jnp.concatenate(pieces, 0)
    kept = lax.dynamic_slice_in_dim(columns, place[3] * piece, piece, 2)
    given = swap(lax.dynamic_slice_in_dim(columns, (1 - place[3]) * piece, piece, 2), BANK, 1)
    return jnp.concatenate([kept, given], 0).reshape(n_bank * samples, 4 * piece).T


def local(latents, shift, scale_mod, head_weight, bank):
    samples, depth = latents.shape
    width = head_weight.shape[1]
    n_gen = lax.axis_size(GEN)
    n_bank = lax.axis_size(BANK)
    evens, odds = list(range(0, n_bank, 2)), list(range(1, n_bank, 2))

    head_other = swap(head_weight, GEN, 1)
    hidden, lent, own, forward, direct = modulate(latents, shift, scale_mod, bank)
    lent = swap(lent, GEN, 2)
    *forward, direct = normalize_sent(forward, direct)
    head_weight, pieces = stage(hidden, head_weight, n_bank)
    bank_unit = normalize(bank)
    lent_part, own_part = project(lent, own, head_weight, head_other)
    returned = swap(lent_part, GEN, 2)
    exact, unit, length = finish_embed(own_part, returned)

    columns = by_feature(hidden, pieces, n_bank)

    forward = [swap(v, BANK, 1) for v in forward]
    direct = swap(direct, BANK, 1)
    beside = [swap(v, GEN, 2) for v in forward]
    forward, beside = join(forward), join(beside)
    early = [forward, swap(forward, GEN, 1)]
    middle = [beside, direct]
    late = [swap(v, GEN, 1) for v in middle]

    line = [unit] + [swap(unit, BANK, m) for m in evens[1:]]
    line = join(line)
    across = swap(line, BANK, 1)
    sums = bank_sums(line, [bank_unit, join(early)])[0]
    sums = bank_sums(line, [join(middle)], sums)[0]
    far = bank_sums(line, [join(late)], sums, samples)
    parts = [swap(v, BANK, m) for m, v in zip(evens[1:], far[1:])]
    near = pair_sums(unit, line, across)
    keep, give = embed_gradient(
        near, far[0], parts, exact, length, bank.shape[0] * n_bank
    )

    given = swap(give, GEN, 2)
    both = join([keep, given])
    high = range(n_bank - 2, n_bank // 2 - 1, -2)
    grads = {0: [keep, given]}
    for m in high:
        grads[m] = [swap(keep, BANK, m)]
    for m in high:
        grads[m].append(swap(given, BANK, m))
    for m in range(n_bank // 2 - 1, 0, -1):
        grads[m] = [swap(both, BANK, m)]
    for m in high:
        ahead = grads[m]
        grads[m + 1] = [swap(v, BANK, 1) for v in ahead]
    grads = [grads[m] for m in evens + odds]
    columns = [columns, swap(columns, GEN, 2)]
    for_core, grads = feature_sums(columns, grads, 1)
    taken = swap(for_core, GEN, 1)
    kept = feature_sums(columns, [[grads]], 0)[0]
    home, away, squares = square_sums(kept, taken, n_gen * n_bank)
    away = swap(away, GEN, 2)
    squares = lax.all_to_all(squares, (GEN, BANK), 0, 0, tiled=True)
    return scaled(home, away, squares, depth * width)


def solution(mesh):
    placed = (
        P((GEN, BANK), None),
        P((GEN, BANK), None),
        P((GEN, BANK), None),
        P(GEN, None),
        P(BANK, None),
    )
    return jax.shard_map(
        lambda *args: local(*args),
        mesh=mesh,
        in_specs=placed,
        out_specs=P((GEN, BANK), None),
        check_vma=False,
    )
```
